32 devices in a mesh: mem: 8 (over z, core), col: 4 (over y, x).
Axes of the slice: x: 2, y: 2, z: 4, core: 2. Of those that a mesh axis runs over, the one named last changes fastest.
Arguments:
- perturbations: bfloat16 [8, 128, 8192], P('mem', None, 'col'), may hold values from -6 to 6
- vertical: bfloat16 [128, 128], replicated, may hold values from -0.5 to 0.5
- blocks: bfloat16 [128, 64, 128], replicated, may hold values from -0.5 to 0.5
- block_scale: float32 [128, 2], replicated, may hold values from 0.5 to 2
- block_cols: int32 [128, 2], replicated, may hold values from 0 to 127
- obs_level: int32 [8192], replicated, may hold values from 0 to 127
- obs_nodes: int32 [8192, 2], replicated, may hold values from 0 to 8191
- obs_weight: float32 [8192], replicated, may hold values from 0.2 to 0.8
- obs_value: float32 [8192], replicated, may hold values from -6 to 6
- obs_precision: float32 [8192], replicated, may hold values from 0.5 to 2
Outputs:
- control: bfloat16 [8, 128, 8192], P('mem', 'col')
- increment: float32 [128, 8192], P('mem', 'col')
The draws below stay inside these ranges and needn't reach their ends.
All inputs are finite; a program needn't handle non-finite values.
Results may differ from the reference program's by a relative error of at most 0.018.
Values may be sent and summed in bfloat16 or wider, within the bound.
No kernel may reach another device: no remote copies, remote signals or barrier semaphores. Data moves between devices by JAX's collectives and lax.ppermute only.
A program may use at most 64 MiB of HBM per device.

```python
import math
import jax
import jax.numpy as jnp
from jax import lax

LEV = 128
NODES = 8192
BLK = 64
KB = 2
ITERS = 2
NOBS = 8192
MEMBERS = 8
NB = 128


def with_ends(values, own_key, smallest, top_value):
    spot = [jax.random.randint(jax.random.fold_in(own_key, axis), (), 0, length) for axis, length in enumerate(values.shape)]
    longest = values.shape.index(max(values.shape))
    next_to = spot[:longest] + [(spot[longest] + 1) % values.shape[longest]] + spot[longest + 1:]
    return values.at[tuple(spot)].set(smallest).at[tuple(next_to)].set(top_value)


def levels(rng, shape, cuts, low, largest):
    factor_of = 1.0
    for position, shards_of in cuts:
        heights = jax.random.uniform(jax.random.fold_in(jax.random.fold_in(rng, 6), position), (shards_of,), jnp.float32, low / len(cuts), largest / len(cuts))
        factor_of = factor_of * jnp.repeat(jnp.exp(heights), shape[position] // shards_of).reshape((-1,) + (1,) * (len(shape) - 1 - position))
    return factor_of


def scatter_about(own_key, shape, scale, most, shards=(), held_as=jnp.bfloat16):
    entries = jax.random.normal(own_key, shape, jnp.float32) * scale
    if len(shards) > 0:
        entries = levels(own_key, shape, shards, -0.22, 0.18) * entries
    return jnp.clip(entries, min=-most, max=most).astype(held_as)


def setup_inputs(seed: int = 0) -> dict:
    arg_keys = jax.random.split(jax.random.key(seed), 11)
    return {
        "perturbations": scatter_about(arg_keys[0], (MEMBERS, LEV, NODES), 1.0, 6.0, ((0, 8), (2, 4))),
        "vertical": scatter_about(arg_keys[1], (LEV, LEV), LEV ** -0.5, 0.5),
        "blocks": scatter_about(arg_keys[2], (NB, BLK, KB * BLK), (KB * BLK) ** -0.5, 0.5),
        "block_scale": jnp.clip(jnp.exp(jax.random.uniform(arg_keys[3], (NB, KB), jnp.float32, math.log(0.5), math.log(2.0))), 0.5, 2.0),
        "block_cols": with_ends(jax.random.randint(arg_keys[4], (NB, KB), 0, NB), jax.random.fold_in(arg_keys[4], 1), 0, NB - 1).astype(jnp.int32),
        "obs_level": with_ends(jax.random.randint(arg_keys[5], (NOBS,), 0, LEV), jax.random.fold_in(arg_keys[5], 1), 0, LEV - 1).astype(jnp.int32),
        "obs_nodes": with_ends(jax.random.randint(arg_keys[6], (NOBS, 2), 0, NODES), jax.random.fold_in(arg_keys[6], 1), 0, NODES - 1).astype(jnp.int32),
        "obs_weight": jnp.clip(jax.random.uniform(arg_keys[7], (NOBS,), jnp.float32, 0.2, 0.8), 0.2, 0.8),
        "obs_value": scatter_about(arg_keys[8], (NOBS,), 1.0, 6.0, (), jnp.float32),
        "obs_precision": jnp.clip(jnp.exp(jax.random.uniform(arg_keys[9], (NOBS,), jnp.float32, math.log(0.5), math.log(2.0))), 0.5, 2.0),
    }


def horizontal_member(field, blocks, block_scale, block_cols):
    rounded = field.astype(jnp.bfloat16).reshape(LEV, NB, BLK)
    picked = jnp.take(rounded, block_cols.reshape(-1), axis=1).reshape(LEV, NB, KB, BLK)
    shaped = blocks.reshape(NB, BLK, KB, BLK)
    terms = jnp.einsum('likj,iakj->lika', picked.astype(jnp.float32), shaped.astype(jnp.float32), precision=lax.Precision.HIGHEST)
    mixed = rounded.astype(jnp.float32) + lax.optimization_barrier(jnp.sum(terms * block_scale[None, :, :, None], axis=2))
    return mixed.reshape(LEV, NODES).astype(jnp.bfloat16)

def horizontal_adjoint_member(moved, blocks, block_scale, block_cols):
    flat = moved.reshape(LEV, NB, BLK)
    shaped = blocks.reshape(NB, BLK, KB, BLK)
    terms = jnp.einsum('lia,iakj->likj', flat.astype(jnp.float32), shaped.astype(jnp.float32), precision=lax.Precision.HIGHEST)
    terms = terms * block_scale[None, :, :, None]
    spread = jnp.zeros((LEV, NB, BLK), jnp.float32).at[:, block_cols.reshape(-1), :].add(terms.reshape(LEV, NB * KB, BLK))
    return (flat.astype(jnp.float32) + spread).reshape(LEV, NODES)

def reference(perturbations, vertical, blocks, block_scale, block_cols, obs_level, obs_nodes, obs_weight, obs_value, obs_precision):
    scale_inv = 1.0 / math.sqrt(MEMBERS)
    first_idx = obs_level * NODES + obs_nodes[:, 0]
    second_idx = obs_level * NODES + obs_nodes[:, 1]

    def forward(field):

        def accumulate(total, pair):
            member_field, member_pert = pair
            mixed = horizontal_member(member_field, blocks, block_scale, block_cols)
            localized = mixed.astype(jnp.float32) + jnp.dot(vertical, mixed, preferred_element_type=jnp.float32)
            return (total + member_pert.astype(jnp.float32) * localized, None)
        total, _ = lax.scan(accumulate, jnp.zeros((LEV, NODES), jnp.float32), (field, perturbations))
        return total * scale_inv

    def adjoint(grad):

        def one_member(member_pert):
            scaled = (member_pert.astype(jnp.float32) * grad * scale_inv).astype(jnp.bfloat16)
            turned = scaled.astype(jnp.float32) + jnp.dot(vertical.T, scaled, preferred_element_type=jnp.float32)
            return horizontal_adjoint_member(turned.astype(jnp.bfloat16), blocks, block_scale, block_cols)
        return lax.map(one_member, perturbations)

    def observe(field):
        flat = field.reshape(-1)
        return obs_weight * flat[first_idx] + (1.0 - obs_weight) * flat[second_idx]

    def spread_obs(errors):
        flat = jnp.zeros((LEV * NODES,), jnp.float32)
        flat = flat.at[first_idx].add(obs_weight * errors).at[second_idx].add((1.0 - obs_weight) * errors)
        return flat.reshape(LEV, NODES)

    def hessian(field):
        return field + adjoint(spread_obs(obs_precision * observe(forward(field))))
    residual = adjoint(spread_obs(obs_precision * obs_value))
    direction = residual
    state = jnp.zeros_like(residual)
    norm_now = jnp.sum(residual * residual)
    for step in range(ITERS):
        image = hessian(direction)
        alpha = norm_now / jnp.sum(direction * image)
        state = state + alpha * direction
        residual = residual - alpha * image
        if step + 1 < ITERS:
            norm_next = jnp.sum(residual * residual)
            direction = residual + norm_next / norm_now * direction
            norm_now = norm_next
    return (state.astype(jnp.bfloat16), forward(state))
```

```python
import functools
import math

import jax
import jax.numpy as jnp
from jax import lax
from jax.experimental import pallas as pl
from jax.experimental.pallas import tpu as pltpu
from jax.sharding import PartitionSpec as P

ITERS = 2
LANES = 128
WIDE = 512
CHUNK = 512
HALF = 256


def one_hot(keys, rows, values):
    n = keys.shape[1]
    parts = []
    for low in range(0, rows, HALF):
        size = min(HALF, rows - low)
        row = lax.broadcasted_iota(jnp.int32, (size, n), 0).astype(jnp.float32).astype(jnp.bfloat16)
        key = jnp.broadcast_to((keys - low).astype(jnp.float32).astype(jnp.bfloat16), (size, n))
        val = jnp.broadcast_to(values, (size, n))
        parts.append(jnp.where(row == key, val, jnp.zeros_like(val)))
    return parts[0] if len(parts) == 1 else jnp.concatenate(parts, axis=0)


def places(level, node, node_lo, levels, ncols):
    wide = min(WIDE, ncols)
    local = node - node_lo
    inside = (local >= 0) & (local < ncols)
    row = jnp.where(inside, (local // wide) * levels + level, -1024)
    lane = jnp.where(inside, local % wide, -1024)
    return row, lane


def adjoint_kernel(
    node_ref, level_ref, n1_ref, n2_ref, weight_ref, err_ref, pert_ref, vert_ref, out_ref, total
):
    levels, ncols = pert_ref.shape
    bands = out_ref.shape[1]
    members = node_ref[1]
    wide = min(WIDE, ncols)
    chunks = ncols // wide
    node_lo = node_ref[0]
    total[...] = jnp.zeros_like(total)

    def step(c, carry):
        level = level_ref[pl.ds(c, 1), :]
        weight = weight_ref[pl.ds(c, 1), :]
        err = err_ref[pl.ds(c, 1), :]
        rows, lanes = [], []
        for ref, w in ((n1_ref, weight), (n2_ref, 1.0 - weight)):
            row, lane = places(level, ref[pl.ds(c, 1), :], node_lo, levels, ncols)
            rows.append(one_hot(row, chunks * levels, (w * err).astype(jnp.bfloat16)))
            lanes.append(one_hot(lane, wide, jnp.ones_like(w).astype(jnp.bfloat16)))
        total[...] += lax.dot_general(
            jnp.concatenate(rows, axis=1),
            jnp.concatenate(lanes, axis=1),
            (((1,), (1,)), ((), ())),
            preferred_element_type=jnp.float32,
        )
        return carry

    lax.fori_loop(0, level_ref.shape[0], step, 0)
    scale_inv = 1.0 / jnp.sqrt(jnp.full((1, wide), members, jnp.int32).astype(jnp.float32))
    for c in range(chunks):
        part = slice(c * wide, (c + 1) * wide)
        grad = total[c * levels : (c + 1) * levels, :]
        scaled = (pert_ref[:, part].astype(jnp.float32) * grad * scale_inv).astype(jnp.bfloat16)
        turned = scaled.astype(jnp.float32) + lax.dot_general(
            vert_ref[...], scaled, (((0,), (0,)), ((), ())), preferred_element_type=jnp.float32
        )
        for b in range(out_ref.shape[0]):
            out_ref[b, :, part] = turned[b * bands : (b + 1) * bands, :].astype(jnp.bfloat16)


def horizontal_kernel(cols_ref, moved_ref, mats_ref, resid_ref, mixed_ref, spread, picked):
    parts, bands, ncols = moved_ref.shape
    pairs = mats_ref.shape[0]
    per_part = ncols // LANES
    half = LANES // 2
    low = lax.broadcasted_iota(jnp.int32, (bands, LANES), 1) < half
    spread[...] = jnp.zeros_like(spread)

    def tile_of(p):
        lane = pl.multiple_of((p % per_part) * LANES, LANES)
        return p // per_part, pl.ds(lane, LANES)

    def scatter(p, carry):
        part, lanes = tile_of(p)
        terms = jnp.dot(moved_ref[part, :, lanes], mats_ref[p], preferred_element_type=jnp.float32)
        for q in range(2):
            term = terms[:, q * LANES : (q + 1) * LANES]
            for k in range(2):
                col = cols_ref[4 * p + 2 * q + k]
                kept = jnp.where(low, term, 0.0) if k == 0 else jnp.where(low, 0.0, term)
                slot = (col & 1) ^ k
                spread[slot, col >> 1] += kept
        return carry

    lax.fori_loop(0, pairs, scatter, 0)

    def join(p, carry):
        part, lanes = tile_of(p)
        resid = (
            moved_ref[part, :, lanes].astype(jnp.float32)
            + spread[0, p]
            + pltpu.roll(spread[1, p], half, 1)
        )
        resid_ref[:, pl.ds(pl.multiple_of(p * LANES, LANES), LANES)] = resid
        picked[0, p] = resid.astype(jnp.bfloat16).astype(jnp.float32)
        picked[1, p] = pltpu.roll(resid, half, 1).astype(jnp.bfloat16).astype(jnp.float32)
        return carry

    lax.fori_loop(0, pairs, join, 0)

    def gather(p, carry):
        part, lanes = tile_of(p)
        sources = []
        for q in range(2):
            first = cols_ref[4 * p + 2 * q]
            second = cols_ref[4 * p + 2 * q + 1]
            sources.append(
                jnp.where(low, picked[first & 1, first >> 1], picked[(second & 1) ^ 1, second >> 1])
            )
        terms = lax.dot_general(
            jnp.concatenate(sources, axis=1).astype(jnp.bfloat16),
            mats_ref[p],
            (((1,), (1,)), ((), ())),
            preferred_element_type=jnp.float32,
        )
        mixed_ref[part, :, lanes] = (picked[0, p] + terms).astype(jnp.bfloat16)
        return carry

    lax.fori_loop(0, pairs, gather, 0)


def forward_kernel(
    node_ref, level_ref, n1_ref, n2_ref, weight_ref, mixed_ref, pert_ref, vert_ref, field_ref, obs_ref, table
):
    levels, ncols = pert_ref.shape
    wide = min(WIDE, ncols)
    chunks = ncols // wide
    node_lo = node_ref[0]
    members = node_ref[1]
    scale_inv = 1.0 / jnp.sqrt(jnp.full((1, wide), members, jnp.int32).astype(jnp.float32))
    for c in range(chunks):
        part = slice(c * wide, (c + 1) * wide)
        mixed = mixed_ref[:, part]
        localized = mixed.astype(jnp.float32) + jnp.dot(
            vert_ref[...], mixed, preferred_element_type=jnp.float32
        )
        field = pert_ref[:, part].astype(jnp.float32) * localized * scale_inv
        field_ref[:, part] = field
        table[c * levels : (c + 1) * levels, :] = field.astype(jnp.bfloat16)

    def step(c, carry):
        level = level_ref[pl.ds(c, 1), :]
        weight = weight_ref[pl.ds(c, 1), :]
        result = jnp.zeros(weight.shape, jnp.float32)
        for ref, w in ((n1_ref, weight), (n2_ref, 1.0 - weight)):
            row, lane = places(level, ref[pl.ds(c, 1), :], node_lo, levels, ncols)
            hot = one_hot(lane, wide, jnp.ones_like(w).astype(jnp.bfloat16))
            lines = jnp.dot(table[...], hot, preferred_element_type=jnp.float32)
            number = lax.broadcasted_iota(jnp.int32, lines.shape, 0)
            kept = jnp.where(number == row, lines, 0.0)
            result = result + w * jnp.sum(kept, axis=0, keepdims=True)
        obs_ref[pl.ds(c, 1), :] = result
        return carry

    lax.fori_loop(0, level_ref.shape[0], step, 0)


def everywhere(x):
    for axis in ("col", "mem"):
        n = lax.axis_size(axis)
        sent = jnp.broadcast_to(x[None], (n,) + x.shape)
        x = jnp.sum(lax.all_to_all(sent, axis, 0, 0, tiled=True), axis=0)
    return x


def per_device(
    perturbations,
    vertical,
    blocks,
    block_scale,
    block_cols,
    obs_level,
    obs_nodes,
    obs_weight,
    obs_value,
    obs_precision,
):
    local_members, levels, ncols = perturbations.shape
    assert local_members == 1
    nblocks, width, depth = blocks.shape
    assert 2 * width == LANES and depth == LANES
    members = local_members * lax.axis_size("mem")
    ncol = lax.axis_size("col")
    nmem = lax.axis_size("mem")
    bands = levels // ncol
    pairs = nblocks // 2
    pert = perturbations[0]
    info = jnp.stack([lax.axis_index("col") * ncols, jnp.int32(members)]).astype(jnp.int32)
    rows = obs_level.shape[0] // CHUNK

    scaled = (blocks.astype(jnp.float32) * jnp.repeat(block_scale, width, axis=1)[:, None, :]).astype(
        jnp.bfloat16
    ).reshape(pairs, 2, width, depth)
    mats = jnp.concatenate(
        [
            jnp.pad(scaled[:, 0], ((0, 0), (0, 0), (0, depth))),
            jnp.pad(scaled[:, 1], ((0, 0), (0, 0), (depth, 0))),
        ],
        axis=1,
    )
    cols = block_cols.reshape(-1)
    level, first, second, weight, value, precision = (
        a.reshape(rows, CHUNK)
        for a in (obs_level, obs_nodes[:, 0], obs_nodes[:, 1], obs_weight, obs_value, obs_precision)
    )

    vmem = pl.BlockSpec(memory_space=pltpu.VMEM)
    smem = pl.BlockSpec(memory_space=pltpu.SMEM)
    wide = min(WIDE, ncols)

    adjoint = pl.pallas_call(
        adjoint_kernel,
        out_shape=jax.ShapeDtypeStruct((ncol, bands, ncols), jnp.bfloat16),
        in_specs=[smem] + [vmem] * 7,
        out_specs=vmem,
        scratch_shapes=[pltpu.VMEM((ncols // wide * levels, wide), jnp.float32)],
        name="adjoint",
    )
    middle = pl.pallas_call(
        horizontal_kernel,
        out_shape=(
            jax.ShapeDtypeStruct((bands, nblocks * width), jnp.float32),
            jax.ShapeDtypeStruct((ncol, bands, ncols), jnp.bfloat16),
        ),
        in_specs=[smem] + [vmem] * 2,
        out_specs=(vmem, vmem),
        scratch_shapes=[
            pltpu.VMEM((2, pairs, bands, LANES), jnp.float32),
            pltpu.VMEM((2, pairs, bands, LANES), jnp.float32),
        ],
        name="horizontal",
    )
    forward = pl.pallas_call(
        forward_kernel,
        out_shape=(
            jax.ShapeDtypeStruct((levels, ncols), jnp.float32),
            jax.ShapeDtypeStruct((rows, CHUNK), jnp.float32),
        ),
        in_specs=[smem] + [vmem] * 7,
        out_specs=(vmem, vmem),
        scratch_shapes=[pltpu.VMEM((ncols // wide * levels, wide), jnp.bfloat16)],
        name="forward",
    )

    def gram(errors):
        sent = adjoint(info, level, first, second, weight, errors, pert, vertical)
        moved = lax.all_to_all(sent, "col", 0, 0, tiled=True)
        resid, mixed = middle(cols, moved, mats)
        columns = lax.all_to_all(mixed, "col", 0, 0, tiled=True).reshape(levels, ncols)
        field, partial = forward(info, level, first, second, weight, columns, pert, vertical)
        return resid, field, everywhere(partial)

    errors = precision * value
    fields, resids = [], []
    shares = []
    for step in range(ITERS):
        resid, field, seen = gram(errors)
        resids.append(resid)
        fields.append(field)
        norm_next = jnp.sum(errors * seen)
        if step == 0:
            guide, image = errors, seen
            mix = [jnp.float32(1.0)]
        else:
            beta = norm_next / norm_now
            guide, image = errors + beta * guide, seen + beta * image
            mix = [beta * m for m in mix] + [jnp.float32(1.0)]
        norm_now = norm_next
        along = jnp.sum(guide * image) + jnp.sum(precision * image * image)
        alpha = norm_now / along
        shares = [s + alpha * m for s, m in zip(shares + [jnp.float32(0.0)], mix)]
        errors = errors - alpha * (guide + precision * image)
    state = sum(c * r for c, r in zip(shares, resids))
    total = sum(c * f for c, f in zip(shares, fields)).astype(jnp.bfloat16)
    pieces = lax.all_to_all(
        total.reshape(nmem, levels // nmem, ncols), "mem", 0, 0, tiled=True
    )
    increment = jnp.sum(pieces.astype(jnp.float32), axis=0)
    return (state.astype(jnp.bfloat16)[None], increment)


def solution(mesh):
    in_specs = (P("mem", None, "col"), P(), P(), P(), P(), P(), P(), P(), P(), P())
    out_specs = (P("mem", "col", None), P("mem", "col"))
    return jax.shard_map(
        per_device, mesh=mesh, in_specs=in_specs, out_specs=out_specs, check_vma=False
    )
```

```python
import math

import jax
import jax.numpy as jnp
from jax import lax
from jax.experimental import pallas as pl
from jax.experimental.pallas import tpu as pltpu
from jax.sharding import PartitionSpec as P

ITERS = 2
LANES = 128
WIDE = 512
CHUNK = 512
HALF = 256
UNROLL = 8


def one_hot(keys, rows, values):
    n = keys.shape[1]
    parts = []
    for low in range(0, rows, HALF):
        size = min(HALF, rows - low)
        row = lax.broadcasted_iota(jnp.int32, (size, n), 0).astype(jnp.float32).astype(jnp.bfloat16)
        key = jnp.broadcast_to((keys - low).astype(jnp.float32).astype(jnp.bfloat16), (size, n))
        val = jnp.broadcast_to(values, (size, n))
        parts.append(jnp.where(row == key, val, jnp.zeros_like(val)))
    return parts[0] if len(parts) == 1 else jnp.concatenate(parts, axis=0)


def places(level, node, node_lo, levels, ncols):
    wide = min(WIDE, ncols)
    local = node - node_lo
    inside = (local >= 0) & (local < ncols)
    row = jnp.where(inside, (local // wide) * levels + level, -1024)
    lane = jnp.where(inside, local % wide, -1024)
    return row, lane


def adjoint_kernel(level_ref, nodes_ref, weight_ref, err_ref, pert_ref, vert_ref, out_ref, total):
    levels, ncols = pert_ref.shape
    bands = out_ref.shape[1]
    members = lax.axis_size("mem")
    wide = min(WIDE, ncols)
    chunks = ncols // wide
    node_lo = lax.axis_index("col") * ncols
    total[...] = jnp.zeros_like(total)

    def step(c, carry):
        span = pl.ds(pl.multiple_of(c * CHUNK, CHUNK), CHUNK)
        level = level_ref[:, span]
        weight = weight_ref[:, span]
        err = err_ref[:, span]
        rows, lanes = [], []
        for which, w in ((0, weight), (1, 1.0 - weight)):
            node = nodes_ref[which : which + 1, span]
            row, lane = places(level, node, node_lo, levels, ncols)
            rows.append(one_hot(row, chunks * levels, (w * err).astype(jnp.bfloat16)))
            lanes.append(one_hot(lane, wide, jnp.ones_like(w).astype(jnp.bfloat16)))
        total[...] += lax.dot_general(
            jnp.concatenate(rows, axis=1),
            jnp.concatenate(lanes, axis=1),
            (((1,), (1,)), ((), ())),
            preferred_element_type=jnp.float32,
        )
        return carry

    lax.fori_loop(0, level_ref.shape[1] // CHUNK, step, 0)
    scale_inv = 1.0 / math.sqrt(members)
    for c in range(chunks):
        part = slice(c * wide, (c + 1) * wide)
        grad = total[c * levels : (c + 1) * levels, :]
        scaled = (pert_ref[:, part].astype(jnp.float32) * grad * scale_inv).astype(jnp.bfloat16)
        turned = scaled.astype(jnp.float32) + lax.dot_general(
            vert_ref[...], scaled, (((0,), (0,)), ((), ())), preferred_element_type=jnp.float32
        )
        for b in range(out_ref.shape[0]):
            out_ref[b, :, part] = turned[b * bands : (b + 1) * bands, :].astype(jnp.bfloat16)


def horizontal_kernel(cols_ref, moved_ref, mats_ref, resid_ref, mixed_ref, terms, first, second, picked):
    parts, bands, ncols = moved_ref.shape
    pairs = mats_ref.shape[0]
    per_part = ncols // LANES
    half = LANES // 2
    lane = lax.broadcasted_iota(jnp.int32, (bands, LANES), 1)
    low = lane < half
    low16 = lane.astype(jnp.float32).astype(jnp.bfloat16) < half
    sums = (first, second)
    for s in sums:
        s[...] = jnp.zeros_like(s)

    def tile_of(p):
        at = pl.multiple_of((p % per_part) * LANES, LANES)
        return p // per_part, pl.ds(at, LANES)

    def product(p, carry):
        part, lanes = tile_of(p)
        both = jnp.dot(moved_ref[part, :, lanes], mats_ref[p], preferred_element_type=jnp.float32)
        terms[2 * p] = both[:, :LANES]
        terms[2 * p + 1] = both[:, LANES:]
        return carry

    lax.fori_loop(0, pairs, product, 0, unroll=UNROLL)

    def scatter(i, carry):
        term = terms[i]
        for k in range(2):
            col = cols_ref[k, i]
            sums[k][(col & 1) ^ k, col >> 1] += term
        return carry

    lax.fori_loop(0, 2 * pairs, scatter, 0, unroll=UNROLL)

    def join(p, carry):
        part, lanes = tile_of(p)
        here = jnp.where(low, first[0, p], second[0, p])
        there = jnp.where(low, first[1, p], second[1, p])
        resid = moved_ref[part, :, lanes].astype(jnp.float32) + here + pltpu.roll(there, half, 1)
        resid_ref[:, pl.ds(pl.multiple_of(p * LANES, LANES), LANES)] = resid
        picked[0, p] = resid.astype(jnp.bfloat16)
        picked[1, p] = pltpu.roll(resid, half, 1).astype(jnp.bfloat16)
        return carry

    lax.fori_loop(0, pairs, join, 0, unroll=UNROLL)

    def gather(p, carry):
        part, lanes = tile_of(p)
        sources = []
        for q in range(2):
            one = cols_ref[0, 2 * p + q]
            two = cols_ref[1, 2 * p + q]
            sources.append(jnp.where(low16, picked[one & 1, one >> 1], picked[(two & 1) ^ 1, two >> 1]))
        both = lax.dot_general(
            jnp.concatenate(sources, axis=1),
            mats_ref[p],
            (((1,), (1,)), ((), ())),
            preferred_element_type=jnp.float32,
        )
        mixed_ref[part, :, lanes] = (picked[0, p].astype(jnp.float32) + both).astype(jnp.bfloat16)
        return carry

    lax.fori_loop(0, pairs, gather, 0, unroll=UNROLL)


def forward_kernel(level_ref, nodes_ref, weight_ref, mixed_ref, pert_ref, vert_ref, field_ref, obs_ref, table):
    levels, ncols = pert_ref.shape
    members = lax.axis_size("mem")
    wide = min(WIDE, ncols)
    chunks = ncols // wide
    node_lo = lax.axis_index("col") * ncols
    core = lax.axis_index("mem") % 2
    scale_inv = 1.0 / math.sqrt(members)
    for c in range(chunks):
        part = slice(c * wide, (c + 1) * wide)
        mixed = mixed_ref[:, part]
        localized = mixed.astype(jnp.float32) + jnp.dot(
            vert_ref[...], mixed, preferred_element_type=jnp.float32
        )
        field = (pert_ref[:, part].astype(jnp.float32) * localized * scale_inv).astype(jnp.bfloat16)
        table[c * levels : (c + 1) * levels, :] = field
        if len(field_ref.shape) == 2:
            field_ref[:, part] = field
        else:
            _, chips, rows, _ = field_ref.shape
            for s in range(2 * chips):
                field_ref[(s % 2) ^ core, s // 2, :, part] = field[s * rows : (s + 1) * rows, :]

    def step(c, carry):
        span = pl.ds(pl.multiple_of(c * CHUNK, CHUNK), CHUNK)
        level = level_ref[:, span]
        weight = weight_ref[:, span]
        result = jnp.zeros(weight.shape, jnp.float32)
        for which, w in ((0, weight), (1, 1.0 - weight)):
            node = nodes_ref[which : which + 1, span]
            row, lane = places(level, node, node_lo, levels, ncols)
            hot = one_hot(lane, wide, jnp.ones_like(w).astype(jnp.bfloat16))
            lines = jnp.dot(table[...], hot, preferred_element_type=jnp.float32)
            number = lax.broadcasted_iota(jnp.int32, lines.shape, 0)
            kept = jnp.where(number == row, lines, 0.0)
            result = result + w * jnp.sum(kept, axis=0, keepdims=True)
        obs_ref[:, span] = result
        return carry

    lax.fori_loop(0, level_ref.shape[1] // CHUNK, step, 0)


def swap(x, axis, offset):
    n = lax.axis_size(axis)
    return lax.ppermute(x, axis, [(i, i ^ offset) for i in range(n)])


def total_over(x, axis, offsets):
    return sum([swap(x, axis, k) for k in offsets], x)


def everywhere(x):
    x = total_over(x, "mem", (1,))
    x = total_over(x, "col", range(1, lax.axis_size("col")))
    return total_over(x, "mem", range(2, lax.axis_size("mem"), 2))


def scatter_members(field):
    if field.ndim == 2:
        nmem = lax.axis_size("mem")
        field = field.reshape(nmem, field.shape[0] // nmem, field.shape[1])
        pieces = lax.all_to_all(field, "mem", 0, 0, tiled=True)
        return jnp.sum(pieces.astype(jnp.float32), axis=0)
    mine = (field[0].astype(jnp.float32) + swap(field[1], "mem", 1).astype(jnp.float32)).astype(jnp.bfloat16)
    chips = mine.shape[0]
    chip = lax.axis_index("mem") // 2
    total = lax.dynamic_index_in_dim(mine, chip, 0, keepdims=False).astype(jnp.float32)
    for k in range(1, chips):
        piece = lax.dynamic_index_in_dim(mine, chip ^ k, 0, keepdims=False)
        total = total + swap(piece, "mem", 2 * k).astype(jnp.float32)
    return total


def per_device(
    perturbations,
    vertical,
    blocks,
    block_scale,
    block_cols,
    obs_level,
    obs_nodes,
    obs_weight,
    obs_value,
    obs_precision,
):
    local_members, levels, ncols = perturbations.shape
    assert local_members == 1
    nblocks, width, depth = blocks.shape
    assert 2 * width == LANES and depth == LANES
    ncol = lax.axis_size("col")
    nmem = lax.axis_size("mem")
    bands = levels // ncol
    pairs = nblocks // 2
    nobs = obs_level.shape[0]
    pert = perturbations[0]

    scaled = (blocks.astype(jnp.float32) * jnp.repeat(block_scale, width, axis=1)[:, None, :]).astype(
        jnp.bfloat16
    ).reshape(pairs, 2, width, depth)
    mats = jnp.concatenate(
        [
            jnp.pad(scaled[:, 0], ((0, 0), (0, 0), (0, depth))),
            jnp.pad(scaled[:, 1], ((0, 0), (0, 0), (depth, 0))),
        ],
        axis=1,
    )
    cols = block_cols.T
    nodes = obs_nodes.T
    level, weight, value, precision = (
        a.reshape(1, nobs) for a in (obs_level, obs_weight, obs_value, obs_precision)
    )

    vmem = pl.BlockSpec(memory_space=pltpu.VMEM)
    smem = pl.BlockSpec(memory_space=pltpu.SMEM)
    wide = min(WIDE, ncols)
    slices = levels // nmem

    adjoint = pl.pallas_call(
        adjoint_kernel,
        out_shape=jax.ShapeDtypeStruct((ncol, bands, ncols), jnp.bfloat16),
        in_specs=[vmem] * 6,
        out_specs=vmem,
        scratch_shapes=[pltpu.VMEM((ncols // wide * levels, wide), jnp.float32)],
        name="adjoint",
    )
    middle = pl.pallas_call(
        horizontal_kernel,
        out_shape=(
            jax.ShapeDtypeStruct((bands, nblocks * width), jnp.float32),
            jax.ShapeDtypeStruct((ncol, bands, ncols), jnp.bfloat16),
        ),
        in_specs=[smem] + [vmem] * 2,
        out_specs=(vmem, vmem),
        scratch_shapes=[
            pltpu.VMEM((2 * pairs, bands, LANES), jnp.float32),
            pltpu.VMEM((2, pairs, bands, LANES), jnp.float32),
            pltpu.VMEM((2, pairs, bands, LANES), jnp.float32),
            pltpu.VMEM((2, pairs, bands, LANES), jnp.bfloat16),
        ],
        name="horizontal",
    )
    field_shape = (2, nmem // 2, slices, ncols) if slices % 16 == 0 else (levels, ncols)
    forward = pl.pallas_call(
        forward_kernel,
        out_shape=(
            jax.ShapeDtypeStruct(field_shape, jnp.bfloat16),
            jax.ShapeDtypeStruct((1, nobs), jnp.float32),
        ),
        in_specs=[vmem] * 6,
        out_specs=(vmem, vmem),
        scratch_shapes=[pltpu.VMEM((ncols // wide * levels, wide), jnp.bfloat16)],
        name="forward",
    )

    def gram(errors):
        sent = adjoint(level, nodes, weight, errors, pert, vertical)
        moved = lax.all_to_all(sent, "col", 0, 0, tiled=True)
        resid, mixed = middle(cols, moved, mats)
        columns = lax.all_to_all(mixed, "col", 0, 0, tiled=True).reshape(levels, ncols)
        field, partial = forward(level, nodes, weight, columns, pert, vertical)
        return resid, scatter_members(field), everywhere(partial)

    errors = precision * value
    fields, resids = [], []
    shares = []
    for step in range(ITERS):
        resid, field, seen = gram(errors)
        resids.append(resid)
        fields.append(field)
        norm_next = jnp.sum(errors * seen)
        if step == 0:
            guide, image = errors, seen
            mix = [jnp.float32(1.0)]
        else:
            beta = norm_next / norm_now
            guide, image = errors + beta * guide, seen + beta * image
            mix = [beta * m for m in mix] + [jnp.float32(1.0)]
        norm_now = norm_next
        along = jnp.sum(guide * image) + jnp.sum(precision * image * image)
        alpha = norm_now / along
        shares = [s + alpha * m for s, m in zip(shares + [jnp.float32(0.0)], mix)]
        errors = errors - alpha * (guide + precision * image)
    state = sum(c * r for c, r in zip(shares, resids))
    increment = sum(c * f for c, f in zip(shares, fields))
    return (state.astype(jnp.bfloat16)[None], increment)


def solution(mesh):
    in_specs = (P("mem", None, "col"), P(), P(), P(), P(), P(), P(), P(), P(), P())
    out_specs = (P("mem", "col", None), P("mem", "col"))
    return jax.shard_map(
        per_device, mesh=mesh, in_specs=in_specs, out_specs=out_specs, check_vma=False
    )
```

```python
import functools
import math

import jax
import jax.numpy as jnp
from jax import lax
from jax.experimental import pallas as pl
from jax.experimental.pallas import tpu as pltpu
from jax.sharding import PartitionSpec as P

ITERS = 2
LANES = 128
WIDE = 256
ROWS = 256
CHUNK = 1024
UNROLL = 8


def grouping(levels, ncols):
    wide = min(WIDE, ncols)
    chunks = ncols // wide
    group = max(8, min(levels, ROWS // chunks))
    return wide, chunks, group


def one_hot(keys, numbers, values):
    key = jnp.broadcast_to(keys.astype(jnp.bfloat16), numbers.shape)
    val = jnp.broadcast_to(values, numbers.shape)
    return jnp.where(numbers == key, val, jnp.zeros_like(val))


def row_numbers(rows, n):
    return lax.broadcasted_iota(jnp.int32, (rows, n), 0).astype(jnp.float32).astype(jnp.bfloat16)


def span_of(c):
    return pl.ds(pl.multiple_of(c * CHUNK, CHUNK), CHUNK)


def total_of(x):
    return jnp.sum(x, axis=1, keepdims=True)


def advance(seen_refs, precision, errors, previous):
    seen = seen_refs[0][...]
    for ref in seen_refs[1:]:
        seen = seen + ref[...]
    norm = total_of(errors * seen)
    if previous is None:
        beta = jnp.zeros_like(norm)
        guide, image = errors, seen
    else:
        beta = norm / previous[2]
        guide, image = errors + beta * previous[0], seen + beta * previous[1]
    along = total_of(guide * image) + total_of(precision * image * image)
    return norm / along, beta, guide, image, norm


def adjoint_kernel(*refs, seen, first):
    starts_ref, keys_ref, weight_ref, precision_ref, err_ref, pert_ref, vert_ref = refs[:7]
    refs = refs[7:]
    levels, ncols = pert_ref.shape
    members = lax.axis_size("mem")
    wide, chunks, group = grouping(levels, ncols)
    rows = chunks * group
    if seen:
        before, refs = (None, refs) if first else ([r[...] for r in refs[:3]], refs[3:])
        seen_refs, refs = refs[:seen], refs[seen:]
        out_ref, new_ref, alpha_ref, beta_ref, guide_ref, image_ref, norm_ref, total, field = refs
        if before is not None:
            before[2] = before[2][:, :1]
        errors, precision = err_ref[...], precision_ref[...]
        alpha, beta, guide, image, norm = advance(seen_refs, precision, errors, before)
        new_ref[...] = errors - alpha * (guide + precision * image)
        guide_ref[...] = guide
        image_ref[...] = image
        for ref, value in ((alpha_ref, alpha), (beta_ref, beta), (norm_ref, norm)):
            ref[...] = jnp.broadcast_to(value, ref.shape)
    else:
        out_ref, new_ref, total, field = refs
        new_ref[...] = precision_ref[...] * err_ref[...]
    bands = out_ref.shape[1]
    numbers = row_numbers(rows, CHUNK)
    places = row_numbers(wide, CHUNK)
    ones = jnp.ones((1, CHUNK), jnp.bfloat16)

    def collect(g, carry):
        total[...] = jnp.zeros_like(total)
        base = (g * rows).astype(jnp.float32)

        def step(c, carry):
            span = span_of(c)
            weight = weight_ref[:, span]
            err = new_ref[:, span]
            above, beside = [], []
            for which, w in ((0, weight), (1, 1.0 - weight)):
                row = keys_ref[2 * which : 2 * which + 1, span] - base
                above.append(one_hot(row, numbers, (w * err).astype(jnp.bfloat16)))
                beside.append(one_hot(keys_ref[2 * which + 1 : 2 * which + 2, span], places, ones))
            total[...] += lax.dot_general(
                jnp.concatenate(above, axis=1),
                jnp.concatenate(beside, axis=1),
                (((1,), (1,)), ((), ())),
                preferred_element_type=jnp.float32,
            )
            return carry

        lax.fori_loop(starts_ref[g] // CHUNK, (starts_ref[g + 1] + CHUNK - 1) // CHUNK, step, 0)
        here = pl.ds(pl.multiple_of(g * group, group), group)
        for c in range(chunks):
            field[here, c * wide : (c + 1) * wide] = total[c * group : (c + 1) * group, :]
        return carry

    lax.fori_loop(0, levels // group, collect, 0)

    scale_inv = 1.0 / math.sqrt(members)
    for c in range(chunks):
        part = slice(c * wide, (c + 1) * wide)
        scaled = (pert_ref[:, part].astype(jnp.float32) * field[:, part] * scale_inv).astype(jnp.bfloat16)
        turned = scaled.astype(jnp.float32) + lax.dot_general(
            vert_ref[...], scaled, (((0,), (0,)), ((), ())), preferred_element_type=jnp.float32
        )
        for b in range(out_ref.shape[0]):
            out_ref[b, :, part] = turned[b * bands : (b + 1) * bands, :].astype(jnp.bfloat16)


def horizontal_kernel(cols_ref, moved_ref, mats_ref, resid_ref, mixed_ref, terms, first, second, picked):
    parts, bands, ncols = moved_ref.shape
    pairs = mats_ref.shape[0]
    per_part = ncols // LANES
    half = LANES // 2
    lane = lax.broadcasted_iota(jnp.int32, (bands, LANES), 1)
    low = lane < half
    low16 = lane.astype(jnp.float32).astype(jnp.bfloat16) < half
    sums = (first, second)
    for s in sums:
        s[...] = jnp.zeros_like(s)

    def tile_of(p):
        at = pl.multiple_of((p % per_part) * LANES, LANES)
        return p // per_part, pl.ds(at, LANES)

    def product(p, carry):
        part, lanes = tile_of(p)
        both = jnp.dot(moved_ref[part, :, lanes], mats_ref[p], preferred_element_type=jnp.float32)
        terms[2 * p] = both[:, :LANES]
        terms[2 * p + 1] = both[:, LANES:]
        return carry

    lax.fori_loop(0, pairs, product, 0, unroll=UNROLL)

    def scatter(i, carry):
        term = terms[i]
        for k in range(2):
            col = cols_ref[k, i]
            sums[k][(col & 1) ^ k, col >> 1] += term
        return carry

    lax.fori_loop(0, 2 * pairs, scatter, 0, unroll=UNROLL)

    def join(p, carry):
        part, lanes = tile_of(p)
        here = jnp.where(low, first[0, p], second[0, p])
        there = jnp.where(low, first[1, p], second[1, p])
        resid = moved_ref[part, :, lanes].astype(jnp.float32) + here + pltpu.roll(there, half, 1)
        resid_ref[:, pl.ds(pl.multiple_of(p * LANES, LANES), LANES)] = resid
        picked[0, p] = resid.astype(jnp.bfloat16)
        picked[1, p] = pltpu.roll(resid, half, 1).astype(jnp.bfloat16)
        return carry

    lax.fori_loop(0, pairs, join, 0, unroll=UNROLL)

    def gather(p, carry):
        part, lanes = tile_of(p)
        sources = []
        for q in range(2):
            one = cols_ref[0, 2 * p + q]
            two = cols_ref[1, 2 * p + q]
            sources.append(jnp.where(low16, picked[one & 1, one >> 1], picked[(two & 1) ^ 1, two >> 1]))
        both = lax.dot_general(
            jnp.concatenate(sources, axis=1),
            mats_ref[p],
            (((1,), (1,)), ((), ())),
            preferred_element_type=jnp.float32,
        )
        mixed_ref[part, :, lanes] = (picked[0, p].astype(jnp.float32) + both).astype(jnp.bfloat16)
        return carry

    lax.fori_loop(0, pairs, gather, 0, unroll=UNROLL)


def forward_kernel(starts_ref, keys_ref, weight_ref, mixed_ref, pert_ref, vert_ref, field_ref, obs_ref):
    levels, ncols = pert_ref.shape
    members = lax.axis_size("mem")
    wide, chunks, group = grouping(levels, ncols)
    rows = chunks * group
    scale_inv = 1.0 / math.sqrt(members)
    for c in range(chunks):
        part = slice(c * wide, (c + 1) * wide)
        mixed = mixed_ref[:, part]
        localized = mixed.astype(jnp.float32) + jnp.dot(
            vert_ref[...], mixed, preferred_element_type=jnp.float32
        )
        field = (pert_ref[:, part].astype(jnp.float32) * localized * scale_inv).astype(jnp.bfloat16)
        for g in range(levels // group):
            field_ref[g, c * group : (c + 1) * group, :] = field[g * group : (g + 1) * group, :]

    obs_ref[...] = jnp.zeros_like(obs_ref)
    places = row_numbers(wide, CHUNK)
    ones = jnp.ones((1, CHUNK), jnp.bfloat16)
    numbers = lax.broadcasted_iota(jnp.int32, (rows, CHUNK), 0).astype(jnp.float32)
    def collect(g, carry):
        base = (g * rows).astype(jnp.float32)

        def step(c, carry):
            span = span_of(c)
            weight = weight_ref[:, span]
            result = obs_ref[:, span]
            for which, w in ((0, weight), (1, 1.0 - weight)):
                row = keys_ref[2 * which : 2 * which + 1, span] - base
                hot = one_hot(keys_ref[2 * which + 1 : 2 * which + 2, span], places, ones)
                lines = jnp.dot(field_ref[g], hot, preferred_element_type=jnp.float32)
                kept = jnp.where(numbers == row, lines, 0.0)
                result = result + w * jnp.sum(kept, axis=0, keepdims=True)
            obs_ref[:, span] = result
            return carry

        lax.fori_loop(starts_ref[g] // CHUNK, (starts_ref[g + 1] + CHUNK - 1) // CHUNK, step, 0)
        return carry

    lax.fori_loop(0, levels // group, collect, 0)


def finish_kernel(*refs, seen, group, wide):
    precision_ref, err_ref, guide_ref, image_ref, norm_ref = refs[:5]
    refs = refs[5:]
    seen_refs, refs = refs[:seen], refs[seen:]
    state_ref, field_ref = refs[-2:]
    refs = refs[:-2]
    steps = len(refs) // 4 + 1
    alphas, betas, rest = refs[: steps - 1], refs[steps - 1 : 2 * steps - 2], refs[2 * steps - 2 :]
    resids, fields = rest[:steps], rest[steps:]
    before = (guide_ref[...], image_ref[...], norm_ref[:, :1])
    alpha, beta, _, _, _ = advance(seen_refs, precision_ref[...], err_ref[...], before)
    alphas = [a[:, :1] for a in alphas] + [alpha]
    betas = [b[:, :1] for b in betas] + [beta]
    mix, shares = [], []
    for a, b in zip(alphas, betas):
        mix = [b * m for m in mix] + [jnp.ones_like(a)]
        shares = [s + a * m for s, m in zip(shares + [jnp.zeros_like(a)], mix)]
    state = shares[0] * resids[0][...]
    for share, resid in zip(shares[1:], resids[1:]):
        state = state + share * resid[...]
    state_ref[...] = state.astype(jnp.bfloat16)
    groups, rows, _ = fields[0].shape
    core = lax.axis_index("mem") % 2
    for g in range(groups):
        total = shares[0] * fields[0][g].astype(jnp.float32)
        for share, field in zip(shares[1:], fields[1:]):
            total = total + share * field[g].astype(jnp.float32)
        total = total.astype(jnp.bfloat16)
        for c in range(rows // group):
            part = slice(c * wide, (c + 1) * wide)
            if len(field_ref.shape) == 2:
                field_ref[g * group : (g + 1) * group, part] = total[c * group : (c + 1) * group, :]
            else:
                size = field_ref.shape[2]
                for s in range(group // size):
                    number = g * (group // size) + s
                    field_ref[(number % 2) ^ core, number // 2, :, part] = total[
                        c * group + s * size : c * group + (s + 1) * size, :
                    ]


def swap(x, axis, offset):
    n = lax.axis_size(axis)
    return lax.ppermute(x, axis, [(i, i ^ offset) for i in range(n)])


def total_over(x, axis, offsets):
    return sum([swap(x, axis, k) for k in offsets], x)


def shares_everywhere(x):
    x = total_over(x, "mem", (1,))
    x = total_over(x, "col", range(1, lax.axis_size("col")))
    return [x] + [swap(x, "mem", k) for k in range(2, lax.axis_size("mem"), 2)]


def scatter_members(field):
    if field.ndim == 2:
        nmem = lax.axis_size("mem")
        field = field.reshape(nmem, field.shape[0] // nmem, field.shape[1])
        pieces = lax.all_to_all(field, "mem", 0, 0, tiled=True)
        return jnp.sum(pieces.astype(jnp.float32), axis=0)
    mine = (field[0].astype(jnp.float32) + swap(field[1], "mem", 1).astype(jnp.float32)).astype(jnp.bfloat16)
    chips = mine.shape[0]
    chip = lax.axis_index("mem") // 2
    total = lax.dynamic_index_in_dim(mine, chip, 0, keepdims=False).astype(jnp.float32)
    for k in range(1, chips):
        piece = lax.dynamic_index_in_dim(mine, chip ^ k, 0, keepdims=False)
        total = total + swap(piece, "mem", 2 * k).astype(jnp.float32)
    return total


def per_device(
    perturbations,
    vertical,
    blocks,
    block_scale,
    block_cols,
    obs_level,
    obs_nodes,
    obs_weight,
    obs_value,
    obs_precision,
):
    local_members, levels, ncols = perturbations.shape
    assert local_members == 1
    nblocks, width, depth = blocks.shape
    assert 2 * width == LANES and depth == LANES
    ncol = lax.axis_size("col")
    nmem = lax.axis_size("mem")
    bands = levels // ncol
    pairs = nblocks // 2
    nodes = nblocks * width
    nobs = obs_level.shape[0]
    pert = perturbations[0]
    wide, chunks, group = grouping(levels, ncols)
    rows = chunks * group
    slices = levels // nmem

    order = obs_level * nobs + jnp.arange(nobs, dtype=jnp.int32)
    both = obs_nodes[:, 0] * nodes + obs_nodes[:, 1]
    order, both, weight, value, precision = lax.sort(
        (order, both, obs_weight, obs_value, obs_precision), num_keys=1, is_stable=False
    )
    level = order // nobs
    keys = []
    for node in (both // nodes, both % nodes):
        local = node - lax.axis_index("col") * ncols
        inside = (local >= 0) & (local < ncols)
        row = (level // group) * rows + (local // wide) * group + level % group
        keys += [jnp.where(inside, row, -(1 << 20)), jnp.where(inside, local % wide, 0)]
    keys = jnp.stack(keys).astype(jnp.float32)
    bounds = jnp.arange(levels // group + 1, dtype=jnp.int32) * group
    starts = jnp.sum((obs_level[None, :] < bounds[:, None]).astype(jnp.int32), axis=1)
    weight, value, precision = (a.reshape(1, nobs) for a in (weight, value, precision))

    scaled = (blocks.astype(jnp.float32) * jnp.repeat(block_scale, width, axis=1)[:, None, :]).astype(
        jnp.bfloat16
    ).reshape(pairs, 2, width, depth)
    mats = jnp.concatenate(
        [
            jnp.pad(scaled[:, 0], ((0, 0), (0, 0), (0, depth))),
            jnp.pad(scaled[:, 1], ((0, 0), (0, 0), (depth, 0))),
        ],
        axis=1,
    )
    cols = block_cols.T

    vmem = pl.BlockSpec(memory_space=pltpu.VMEM)
    smem = pl.BlockSpec(memory_space=pltpu.SMEM)
    vector = jax.ShapeDtypeStruct((1, nobs), jnp.float32)
    number = jax.ShapeDtypeStruct((1, LANES), jnp.float32)
    moved_shape = jax.ShapeDtypeStruct((ncol, bands, ncols), jnp.bfloat16)

    def adjoint(errors, seen, before):
        count = len(seen)
        outs = (moved_shape, vector) + ((number, number, vector, vector, number) if count else ())
        extra = (list(before) if before is not None else []) + list(seen)
        return pl.pallas_call(
            functools.partial(adjoint_kernel, seen=count, first=before is None),
            out_shape=outs,
            in_specs=[smem] + [vmem] * (6 + len(extra)),
            out_specs=(vmem,) * len(outs),
            scratch_shapes=[
                pltpu.VMEM((rows, wide), jnp.float32),
                pltpu.VMEM((levels, ncols), jnp.float32),
            ],
            name="adjoint",
        )(starts, keys, weight, precision, errors, pert, vertical, *extra)

    middle = pl.pallas_call(
        horizontal_kernel,
        out_shape=(jax.ShapeDtypeStruct((bands, nodes), jnp.float32), moved_shape),
        in_specs=[smem] + [vmem] * 2,
        out_specs=(vmem, vmem),
        scratch_shapes=[
            pltpu.VMEM((2 * pairs, bands, LANES), jnp.float32),
            pltpu.VMEM((2, pairs, bands, LANES), jnp.float32),
            pltpu.VMEM((2, pairs, bands, LANES), jnp.float32),
            pltpu.VMEM((2, pairs, bands, LANES), jnp.bfloat16),
        ],
        name="horizontal",
    )
    forward = pl.pallas_call(
        forward_kernel,
        out_shape=(
            jax.ShapeDtypeStruct((levels // group, rows, wide), jnp.bfloat16),
            vector,
        ),
        in_specs=[smem] + [vmem] * 5,
        out_specs=(vmem, vmem),
        name="forward",
    )

    errors, seen, before = value, (), None
    alphas, betas, fields, resids = [], [], [], []
    for step in range(ITERS):
        if step == 0:
            sent, errors = adjoint(errors, seen, None)
        else:
            sent, errors, alpha, beta, *before = adjoint(errors, seen, before)
            alphas.append(alpha)
            betas.append(beta)
        moved = lax.all_to_all(sent, "col", 0, 0, tiled=True)
        resid, mixed = middle(cols, moved, mats)
        columns = lax.all_to_all(mixed, "col", 0, 0, tiled=True).reshape(levels, ncols)
        field, partial = forward(starts, keys, weight, columns, pert, vertical)
        seen = shares_everywhere(partial)
        resids.append(resid)
        fields.append(field)

    split = slices % 16 == 0 and group % slices == 0
    field_shape = (2, nmem // 2, slices, ncols) if split else (levels, ncols)
    args = [precision, errors, *before, *seen, *alphas, *betas, *resids, *fields]
    state, total = pl.pallas_call(
        functools.partial(finish_kernel, seen=len(seen), group=group, wide=wide),
        out_shape=(
            jax.ShapeDtypeStruct((bands, nodes), jnp.bfloat16),
            jax.ShapeDtypeStruct(field_shape, jnp.bfloat16),
        ),
        in_specs=[vmem] * len(args),
        out_specs=(vmem, vmem),
        name="finish",
    )(*args)
    return (state[None], scatter_members(total))


def solution(mesh):
    in_specs = (P("mem", None, "col"), P(), P(), P(), P(), P(), P(), P(), P(), P())
    out_specs = (P("mem", "col", None), P("mem", "col"))
    return jax.shard_map(
        per_device, mesh=mesh, in_specs=in_specs, out_specs=out_specs, check_vma=False
    )
```

```python
import functools
import math

import jax
import jax.numpy as jnp
from jax import lax
from jax.experimental import pallas as pl
from jax.experimental.pallas import tpu as pltpu
from jax.sharding import PartitionSpec as P

ITERS = 2
LANES = 128
WIDE = 256
ROWS = 256
CHUNK = 1024
UNROLL = 8
VMEM_BYTES = 24 << 20


def grouping(levels, ncols):
    wide = min(WIDE, ncols)
    chunks = ncols // wide
    group = max(8, min(levels, ROWS // chunks))
    return wide, chunks, group


def one_hot(keys, numbers, values):
    key = jnp.broadcast_to(keys.astype(jnp.bfloat16), numbers.shape)
    val = jnp.broadcast_to(values, numbers.shape)
    return jnp.where(numbers == key, val, jnp.zeros_like(val))


def row_numbers(rows, n):
    return lax.broadcasted_iota(jnp.int32, (rows, n), 0).astype(jnp.float32).astype(jnp.bfloat16)


def span_of(c):
    return pl.ds(pl.multiple_of(c * CHUNK, CHUNK), CHUNK)


def total_of(x):
    return jnp.sum(x, axis=1, keepdims=True)


def advance(seen_refs, precision, errors, previous):
    seen = seen_refs[0][...]
    for ref in seen_refs[1:]:
        seen = seen + ref[...]
    norm = total_of(errors * seen)
    if previous is None:
        beta = jnp.zeros_like(norm)
        guide, image = errors, seen
    else:
        beta = norm / previous[2]
        guide, image = errors + beta * previous[0], seen + beta * previous[1]
    along = total_of(guide * image) + total_of(precision * image * image)
    return norm / along, beta, guide, image, norm


def adjoint_kernel(*refs, seen, first):
    starts_ref, keys_ref, weight_ref, precision_ref, err_ref, pert_ref, vert_ref = refs[:7]
    refs = refs[7:]
    levels, ncols = pert_ref.shape
    members = lax.axis_size("mem")
    wide, chunks, group = grouping(levels, ncols)
    rows = chunks * group
    if seen:
        before, refs = (None, refs) if first else ([r[...] for r in refs[:3]], refs[3:])
        seen_refs, refs = refs[:seen], refs[seen:]
        out_ref, new_ref, alpha_ref, beta_ref, guide_ref, image_ref, norm_ref, total, field = refs
        if before is not None:
            before[2] = before[2][:, :1]
        errors, precision = err_ref[...], precision_ref[...]
        alpha, beta, guide, image, norm = advance(seen_refs, precision, errors, before)
        new_ref[...] = errors - alpha * (guide + precision * image)
        guide_ref[...] = guide
        image_ref[...] = image
        for ref, value in ((alpha_ref, alpha), (beta_ref, beta), (norm_ref, norm)):
            ref[...] = jnp.broadcast_to(value, ref.shape)
    else:
        out_ref, new_ref, total, field = refs
        new_ref[...] = precision_ref[...] * err_ref[...]
    bands = out_ref.shape[1]
    numbers = row_numbers(rows, CHUNK)
    places = row_numbers(wide, CHUNK)
    ones = jnp.ones((1, CHUNK), jnp.bfloat16)

    def collect(g, carry):
        total[...] = jnp.zeros_like(total)
        base = (g * rows).astype(jnp.float32)

        def step(c, carry):
            span = span_of(c)
            weight = weight_ref[:, span]
            err = new_ref[:, span]
            above, beside = [], []
            for which, w in ((0, weight), (1, 1.0 - weight)):
                row = keys_ref[2 * which : 2 * which + 1, span] - base
                above.append(one_hot(row, numbers, (w * err).astype(jnp.bfloat16)))
                beside.append(one_hot(keys_ref[2 * which + 1 : 2 * which + 2, span], places, ones))
            total[...] += lax.dot_general(
                jnp.concatenate(above, axis=1),
                jnp.concatenate(beside, axis=1),
                (((1,), (1,)), ((), ())),
                preferred_element_type=jnp.float32,
            )
            return carry

        lax.fori_loop(starts_ref[g] // CHUNK, (starts_ref[g + 1] + CHUNK - 1) // CHUNK, step, 0)
        here = pl.ds(pl.multiple_of(g * group, group), group)
        for c in range(chunks):
            field[here, c * wide : (c + 1) * wide] = total[c * group : (c + 1) * group, :]
        return carry

    lax.fori_loop(0, levels // group, collect, 0)

    scale_inv = 1.0 / math.sqrt(members)
    for c in range(chunks):
        part = slice(c * wide, (c + 1) * wide)
        scaled = (pert_ref[:, part].astype(jnp.float32) * field[:, part] * scale_inv).astype(jnp.bfloat16)
        turned = scaled.astype(jnp.float32) + lax.dot_general(
            vert_ref[...], scaled, (((0,), (0,)), ((), ())), preferred_element_type=jnp.float32
        )
        for b in range(out_ref.shape[0]):
            out_ref[b, :, part] = turned[b * bands : (b + 1) * bands, :].astype(jnp.bfloat16)


def horizontal_kernel(cols_ref, moved_ref, mats_ref, resid_ref, mixed_ref, terms, first, second, picked):
    parts, bands, ncols = moved_ref.shape
    pairs = mats_ref.shape[0]
    per_part = ncols // LANES
    half = LANES // 2
    lane = lax.broadcasted_iota(jnp.int32, (bands, LANES), 1)
    low = lane < half
    low16 = lane.astype(jnp.float32).astype(jnp.bfloat16) < half
    sums = (first, second)
    for s in sums:
        s[...] = jnp.zeros_like(s)

    def tile_of(p):
        at = pl.multiple_of((p % per_part) * LANES, LANES)
        return p // per_part, pl.ds(at, LANES)

    def product(p, carry):
        part, lanes = tile_of(p)
        both = jnp.dot(moved_ref[part, :, lanes], mats_ref[p], preferred_element_type=jnp.float32)
        terms[2 * p] = both[:, :LANES]
        terms[2 * p + 1] = both[:, LANES:]
        return carry

    lax.fori_loop(0, pairs, product, 0, unroll=UNROLL)

    def scatter(i, carry):
        term = terms[i]
        for k in range(2):
            col = cols_ref[k, i]
            sums[k][(col & 1) ^ k, col >> 1] += term
        return carry

    lax.fori_loop(0, 2 * pairs, scatter, 0, unroll=UNROLL)

    def join(p, carry):
        part, lanes = tile_of(p)
        here = jnp.where(low, first[0, p], second[0, p])
        there = jnp.where(low, first[1, p], second[1, p])
        resid = moved_ref[part, :, lanes].astype(jnp.float32) + here + pltpu.roll(there, half, 1)
        resid_ref[:, pl.ds(pl.multiple_of(p * LANES, LANES), LANES)] = resid
        picked[0, p] = resid.astype(jnp.bfloat16)
        picked[1, p] = pltpu.roll(resid, half, 1).astype(jnp.bfloat16)
        return carry

    lax.fori_loop(0, pairs, join, 0, unroll=UNROLL)

    def gather(p, carry):
        part, lanes = tile_of(p)
        sources = []
        for q in range(2):
            one = cols_ref[0, 2 * p + q]
            two = cols_ref[1, 2 * p + q]
            sources.append(jnp.where(low16, picked[one & 1, one >> 1], picked[(two & 1) ^ 1, two >> 1]))
        both = lax.dot_general(
            jnp.concatenate(sources, axis=1),
            mats_ref[p],
            (((1,), (1,)), ((), ())),
            preferred_element_type=jnp.float32,
        )
        mixed_ref[part, :, lanes] = (picked[0, p].astype(jnp.float32) + both).astype(jnp.bfloat16)
        return carry

    lax.fori_loop(0, pairs, gather, 0, unroll=UNROLL)


def forward_kernel(starts_ref, keys_ref, weight_ref, mixed_ref, pert_ref, vert_ref, field_ref, obs_ref):
    levels, ncols = pert_ref.shape
    members = lax.axis_size("mem")
    wide, chunks, group = grouping(levels, ncols)
    rows = chunks * group
    scale_inv = 1.0 / math.sqrt(members)
    for c in range(chunks):
        part = slice(c * wide, (c + 1) * wide)
        mixed = mixed_ref[:, part]
        localized = mixed.astype(jnp.float32) + jnp.dot(
            vert_ref[...], mixed, preferred_element_type=jnp.float32
        )
        field = (pert_ref[:, part].astype(jnp.float32) * localized * scale_inv).astype(jnp.bfloat16)
        for g in range(levels // group):
            field_ref[g, c * group : (c + 1) * group, :] = field[g * group : (g + 1) * group, :]

    obs_ref[...] = jnp.zeros_like(obs_ref)
    places = row_numbers(wide, CHUNK)
    ones = jnp.ones((1, CHUNK), jnp.bfloat16)
    numbers = lax.broadcasted_iota(jnp.int32, (rows, CHUNK), 0).astype(jnp.float32)
    def collect(g, carry):
        base = (g * rows).astype(jnp.float32)

        def step(c, carry):
            span = span_of(c)
            weight = weight_ref[:, span]
            result = obs_ref[:, span]
            for which, w in ((0, weight), (1, 1.0 - weight)):
                row = keys_ref[2 * which : 2 * which + 1, span] - base
                hot = one_hot(keys_ref[2 * which + 1 : 2 * which + 2, span], places, ones)
                lines = jnp.dot(field_ref[g], hot, preferred_element_type=jnp.float32)
                kept = jnp.where(numbers == row, lines, 0.0)
                result = result + w * jnp.sum(kept, axis=0, keepdims=True)
            obs_ref[:, span] = result
            return carry

        lax.fori_loop(starts_ref[g] // CHUNK, (starts_ref[g + 1] + CHUNK - 1) // CHUNK, step, 0)
        return carry

    lax.fori_loop(0, levels // group, collect, 0)


def finish_kernel(*refs, seen, group, wide):
    precision_ref, err_ref, guide_ref, image_ref, norm_ref = refs[:5]
    refs = refs[5:]
    seen_refs, refs = refs[:seen], refs[seen:]
    state_ref, field_ref = refs[-2:]
    refs = refs[:-2]
    steps = len(refs) // 4 + 1
    alphas, betas, rest = refs[: steps - 1], refs[steps - 1 : 2 * steps - 2], refs[2 * steps - 2 :]
    resids, fields = rest[:steps], rest[steps:]
    before = (guide_ref[...], image_ref[...], norm_ref[:, :1])
    alpha, beta, _, _, _ = advance(seen_refs, precision_ref[...], err_ref[...], before)
    alphas = [a[:, :1] for a in alphas] + [alpha]
    betas = [b[:, :1] for b in betas] + [beta]
    mix, shares = [], []
    for a, b in zip(alphas, betas):
        mix = [b * m for m in mix] + [jnp.ones_like(a)]
        shares = [s + a * m for s, m in zip(shares + [jnp.zeros_like(a)], mix)]
    state = shares[0] * resids[0][...]
    for share, resid in zip(shares[1:], resids[1:]):
        state = state + share * resid[...]
    state_ref[...] = state.astype(jnp.bfloat16)
    groups, rows, _ = fields[0].shape
    core = lax.axis_index("mem") % 2
    for g in range(groups):
        total = shares[0] * fields[0][g].astype(jnp.float32)
        for share, field in zip(shares[1:], fields[1:]):
            total = total + share * field[g].astype(jnp.float32)
        total = total.astype(jnp.bfloat16)
        for c in range(rows // group):
            part = slice(c * wide, (c + 1) * wide)
            if len(field_ref.shape) == 2:
                field_ref[g * group : (g + 1) * group, part] = total[c * group : (c + 1) * group, :]
            else:
                size = field_ref.shape[2]
                for s in range(group // size):
                    number = g * (group // size) + s
                    field_ref[(number % 2) ^ core, number // 2, :, part] = total[
                        c * group + s * size : c * group + (s + 1) * size, :
                    ]


def local_call(kernel, outs, args, name, scratch=(), scalars=1):
    vmem = pl.BlockSpec(memory_space=pltpu.VMEM)
    smem = pl.BlockSpec(memory_space=pltpu.SMEM)
    kept = [a if i < scalars else pltpu.with_memory_space_constraint(a, pltpu.VMEM) for i, a in enumerate(args)]
    return pl.pallas_call(
        kernel,
        out_shape=tuple(pltpu.VMEM(o.shape, o.dtype) for o in outs),
        in_specs=[smem] * scalars + [vmem] * (len(args) - scalars),
        out_specs=(vmem,) * len(outs),
        scratch_shapes=list(scratch),
        compiler_params=pltpu.CompilerParams(vmem_limit_bytes=VMEM_BYTES),
        name=name,
    )(*kept)


def swap(x, axis, offset):
    n = lax.axis_size(axis)
    return lax.ppermute(x, axis, [(i, i ^ offset) for i in range(n)])


def total_over(x, axis, offsets):
    return sum([swap(x, axis, k) for k in offsets], x)


def shares_everywhere(x):
    x = total_over(x, "mem", (1,))
    x = total_over(x, "col", range(1, lax.axis_size("col")))
    return [x] + [swap(x, "mem", k) for k in range(2, lax.axis_size("mem"), 2)]


def scatter_members(field):
    if field.ndim == 2:
        nmem = lax.axis_size("mem")
        field = field.reshape(nmem, field.shape[0] // nmem, field.shape[1])
        pieces = lax.all_to_all(field, "mem", 0, 0, tiled=True)
        return jnp.sum(pieces.astype(jnp.float32), axis=0)
    mine = (field[0].astype(jnp.float32) + swap(field[1], "mem", 1).astype(jnp.float32)).astype(jnp.bfloat16)
    chips = mine.shape[0]
    chip = lax.axis_index("mem") // 2
    total = lax.dynamic_index_in_dim(mine, chip, 0, keepdims=False).astype(jnp.float32)
    for k in range(1, chips):
        piece = lax.dynamic_index_in_dim(mine, chip ^ k, 0, keepdims=False)
        total = total + swap(piece, "mem", 2 * k).astype(jnp.float32)
    return total


def per_device(
    perturbations,
    vertical,
    blocks,
    block_scale,
    block_cols,
    obs_level,
    obs_nodes,
    obs_weight,
    obs_value,
    obs_precision,
):
    local_members, levels, ncols = perturbations.shape
    assert local_members == 1
    nblocks, width, depth = blocks.shape
    assert 2 * width == LANES and depth == LANES
    ncol = lax.axis_size("col")
    nmem = lax.axis_size("mem")
    bands = levels // ncol
    pairs = nblocks // 2
    nodes = nblocks * width
    nobs = obs_level.shape[0]
    pert = perturbations[0]
    wide, chunks, group = grouping(levels, ncols)
    rows = chunks * group
    slices = levels // nmem

    order = obs_level * nobs + jnp.arange(nobs, dtype=jnp.int32)
    both = obs_nodes[:, 0] * nodes + obs_nodes[:, 1]
    order, both, weight, value, precision = lax.sort(
        (order, both, obs_weight, obs_value, obs_precision), num_keys=1, is_stable=False
    )
    level = order // nobs
    keys = []
    for node in (both // nodes, both % nodes):
        local = node - lax.axis_index("col") * ncols
        inside = (local >= 0) & (local < ncols)
        row = (level // group) * rows + (local // wide) * group + level % group
        keys += [jnp.where(inside, row, -(1 << 20)), jnp.where(inside, local % wide, 0)]
    keys = jnp.stack(keys).astype(jnp.float32)
    bounds = jnp.arange(levels // group + 1, dtype=jnp.int32) * group
    starts = jnp.sum((obs_level[None, :] < bounds[:, None]).astype(jnp.int32), axis=1)
    weight, value, precision = (a.reshape(1, nobs) for a in (weight, value, precision))

    scaled = (blocks.astype(jnp.float32) * jnp.repeat(block_scale, width, axis=1)[:, None, :]).astype(
        jnp.bfloat16
    ).reshape(pairs, 2, width, depth)
    mats = jnp.concatenate(
        [
            jnp.pad(scaled[:, 0], ((0, 0), (0, 0), (0, depth))),
            jnp.pad(scaled[:, 1], ((0, 0), (0, 0), (depth, 0))),
        ],
        axis=1,
    )
    cols = block_cols.T

    vector = jax.ShapeDtypeStruct((1, nobs), jnp.float32)
    number = jax.ShapeDtypeStruct((1, LANES), jnp.float32)
    moved_shape = jax.ShapeDtypeStruct((ncol, bands, ncols), jnp.bfloat16)

    def adjoint(errors, seen, before):
        count = len(seen)
        outs = (moved_shape, vector) + ((number, number, vector, vector, number) if count else ())
        extra = (list(before) if before is not None else []) + list(seen)
        return local_call(
            functools.partial(adjoint_kernel, seen=count, first=before is None),
            outs,
            [starts, keys, weight, precision, errors, pert, vertical, *extra],
            "adjoint",
            [pltpu.VMEM((rows, wide), jnp.float32), pltpu.VMEM((levels, ncols), jnp.float32)],
        )

    def middle(moved):
        return local_call(
            horizontal_kernel,
            (jax.ShapeDtypeStruct((bands, nodes), jnp.float32), moved_shape),
            [cols, moved, mats],
            "horizontal",
            [
                pltpu.VMEM((2 * pairs, bands, LANES), jnp.float32),
                pltpu.VMEM((2, pairs, bands, LANES), jnp.float32),
                pltpu.VMEM((2, pairs, bands, LANES), jnp.float32),
                pltpu.VMEM((2, pairs, bands, LANES), jnp.bfloat16),
            ],
        )

    def forward(columns):
        field = jax.ShapeDtypeStruct((levels // group, rows, wide), jnp.bfloat16)
        return local_call(
            forward_kernel, (field, vector), [starts, keys, weight, columns, pert, vertical], "forward"
        )

    errors, seen, before = value, (), None
    alphas, betas, fields, resids = [], [], [], []
    for step in range(ITERS):
        if step == 0:
            sent, errors = adjoint(errors, seen, None)
        else:
            sent, errors, alpha, beta, *before = adjoint(errors, seen, before)
            alphas.append(alpha)
            betas.append(beta)
        moved = lax.all_to_all(sent, "col", 0, 0, tiled=True)
        resid, mixed = middle(moved)
        columns = lax.all_to_all(mixed, "col", 0, 0, tiled=True).reshape(levels, ncols)
        field, partial = forward(columns)
        seen = shares_everywhere(partial)
        resids.append(resid)
        fields.append(field)

    split = slices % 16 == 0 and group % slices == 0
    field_shape = (2, nmem // 2, slices, ncols) if split else (levels, ncols)
    args = [precision, errors, *before, *seen, *alphas, *betas, *resids, *fields]
    state, total = local_call(
        functools.partial(finish_kernel, seen=len(seen), group=group, wide=wide),
        (
            jax.ShapeDtypeStruct((bands, nodes), jnp.bfloat16),
            jax.ShapeDtypeStruct(field_shape, jnp.bfloat16),
        ),
        args,
        "finish",
        scalars=0,
    )
    return (state[None], scatter_members(total))


def solution(mesh):
    in_specs = (P("mem", None, "col"), P(), P(), P(), P(), P(), P(), P(), P(), P())
    out_specs = (P("mem", "col", None), P("mem", "col"))
    return jax.shard_map(
        per_device, mesh=mesh, in_specs=in_specs, out_specs=out_specs, check_vma=False
    )
```

```python
import functools
import math

import jax
import jax.numpy as jnp
from jax import lax
from jax.experimental import pallas as pl
from jax.experimental.pallas import tpu as pltpu
from jax.sharding import PartitionSpec as P

ITERS = 2
LANES = 128
SUBLANES = 16
WIDE = 256
ROWS = 256
FIRST = 768
SECOND = 256
TILES = 8
VMEM_BYTES = 24 << 20


def grouping(levels, ncols):
    wide = min(WIDE, ncols)
    chunks = ncols // wide
    group = max(8, min(levels, ROWS // chunks))
    return wide, chunks, group


def one_hot(keys, numbers, values):
    key = jnp.broadcast_to(keys.astype(jnp.bfloat16), numbers.shape)
    val = jnp.broadcast_to(values, numbers.shape)
    return jnp.where(numbers == key, val, jnp.zeros_like(val))


def row_numbers(rows, n):
    return lax.broadcasted_iota(jnp.int32, (rows, n), 0).astype(jnp.float32).astype(jnp.bfloat16)


def runs_of(starts_ref, g, mine, ncol):
    runs = [(0, starts_ref[(g * ncol + mine) * ncol], starts_ref[(g * ncol + mine + 1) * ncol])]
    for other in range(ncol):
        at = (g * ncol + other) * ncol + mine
        runs.append((1, starts_ref[at], starts_ref[at + 1]))
    return runs


def width_of(which):
    return SECOND if which else FIRST


def trips_of(runs):
    trips = jnp.int32(0)
    for which, low, end in runs:
        need = (end - (low // LANES) * LANES + width_of(which) - 1) // width_of(which)
        trips = jnp.maximum(trips, jnp.where(end > low, need, 0))
    return trips


def window_of(run, trip, nobs):
    which, low, end = run
    width = width_of(which)
    first = (low // LANES) * LANES + trip * width
    base = pl.multiple_of(jnp.minimum(first, nobs - width), LANES)
    place = base + lax.broadcasted_iota(jnp.int32, (1, width), 1)
    valid = (place >= jnp.maximum(low, first)) & (place < jnp.minimum(end, first + width))
    return pl.ds(base, width), valid


def total_of(x):
    return jnp.sum(x, axis=1, keepdims=True)


def advance(seen_refs, precision, errors, previous):
    seen = seen_refs[0][...]
    for ref in seen_refs[1:]:
        seen = seen + ref[...]
    norm = total_of(errors * seen)
    if previous is None:
        beta = jnp.zeros_like(norm)
        guide, image = errors, seen
    else:
        beta = norm / previous[2]
        guide, image = errors + beta * previous[0], seen + beta * previous[1]
    along = total_of(guide * image) + total_of(precision * image * image)
    return norm / along, beta, guide, image, norm


def adjoint_kernel(*refs, seen, first):
    starts_ref, pert_hbm, vert_hbm, keys_ref, weight_ref, precision_ref, err_ref = refs[:7]
    pert_ref, vert_ref, sems = refs[-3:]
    refs = refs[7:-3]
    levels, ncols = pert_ref.shape
    copies = [
        pltpu.make_async_copy(pert_hbm, pert_ref, sems.at[0]),
        pltpu.make_async_copy(vert_hbm, vert_ref, sems.at[1]),
    ]
    for copy in copies:
        copy.start()
    members = lax.axis_size("mem")
    wide, chunks, group = grouping(levels, ncols)
    rows = chunks * group
    if seen:
        before, refs = (None, refs) if first else ([r[...] for r in refs[:3]], refs[3:])
        seen_refs, refs = refs[:seen], refs[seen:]
        out_ref, new_ref, alpha_ref, beta_ref, guide_ref, image_ref, norm_ref, total, field = refs
        if before is not None:
            before[2] = before[2][:, :1]
        errors, precision = err_ref[...], precision_ref[...]
        alpha, beta, guide, image, norm = advance(seen_refs, precision, errors, before)
        new_ref[...] = errors - alpha * (guide + precision * image)
        guide_ref[...] = guide
        image_ref[...] = image
        for ref, value in ((alpha_ref, alpha), (beta_ref, beta), (norm_ref, norm)):
            ref[...] = jnp.broadcast_to(value, ref.shape)
    else:
        out_ref, new_ref, total, field = refs
        new_ref[...] = precision_ref[...] * err_ref[...]
    bands = out_ref.shape[1]
    nobs = weight_ref.shape[1]
    ncol = lax.axis_size("col")
    mine = lax.axis_index("col")

    def collect(g, carry):
        total[...] = jnp.zeros_like(total)
        runs = runs_of(starts_ref, g, mine, ncol)

        def step(trip, carry):
            above, beside = [], []
            for run in runs:
                which = run[0]
                span, valid = window_of(run, trip, nobs)
                weight = weight_ref[:, span]
                weight = 1.0 - weight if which else weight
                row = jnp.where(valid, keys_ref[2 * which : 2 * which + 1, span], -1.0)
                lane = keys_ref[2 * which + 1 : 2 * which + 2, span]
                width = width_of(which)
                above.append(one_hot(row, row_numbers(rows, width), (weight * new_ref[:, span]).astype(jnp.bfloat16)))
                beside.append(one_hot(lane, row_numbers(wide, width), jnp.ones((1, width), jnp.bfloat16)))
            total[...] += lax.dot_general(
                jnp.concatenate(above, axis=1),
                jnp.concatenate(beside, axis=1),
                (((1,), (1,)), ((), ())),
                preferred_element_type=jnp.float32,
            )
            return carry

        lax.fori_loop(0, trips_of(runs), step, 0)
        here = pl.ds(pl.multiple_of(g * group, group), group)
        for c in range(chunks):
            field[here, c * wide : (c + 1) * wide] = total[c * group : (c + 1) * group, :]
        return carry

    lax.fori_loop(0, levels // group, collect, 0)

    for copy in copies:
        copy.wait()
    scale_inv = 1.0 / math.sqrt(members)
    for c in range(chunks):
        part = slice(c * wide, (c + 1) * wide)
        scaled = (pert_ref[:, part].astype(jnp.float32) * field[:, part] * scale_inv).astype(jnp.bfloat16)
        turned = scaled.astype(jnp.float32) + lax.dot_general(
            vert_ref[...], scaled, (((0,), (0,)), ((), ())), preferred_element_type=jnp.float32
        )
        for b in range(out_ref.shape[0]):
            out_ref[b, :, part] = turned[b * bands : (b + 1) * bands, :].astype(jnp.bfloat16)


def horizontal_kernel(
    spots_ref, moved_ref, mats_ref, resid_ref, mixed_ref, terms, first, second, picked
):
    parts, bands, ncols = moved_ref.shape
    pairs = mats_ref.shape[0]
    per_part = ncols // LANES
    group = terms.shape[1] // 2
    half = LANES // 2
    lane = lax.broadcasted_iota(jnp.int32, (bands, LANES), 1)
    low = lane < half
    low16 = lane.astype(jnp.float32).astype(jnp.bfloat16) < half
    sums = (first, second)

    for s in sums:
        s[...] = jnp.zeros_like(s)

    def tiles(part, at, body):
        for u in range(group):
            lanes = pl.ds(pl.multiple_of((at + u) * LANES, LANES), LANES)
            body(u, part * per_part + at + u, lanes)

    def over(part, function):
        lax.fori_loop(0, per_part // group, lambda n, c: function(part, n * group, n % 2) or c, 0)

    def products(part, at, slot):
        def one(u, p, lanes):
            tile = moved_ref[part, :, lanes]
            none = jnp.zeros_like(tile)
            tall = jnp.concatenate([jnp.where(low16, tile, none), jnp.where(low16, none, tile)], axis=0)
            both = jnp.dot(tall, mats_ref[p], preferred_element_type=jnp.float32)
            terms[slot, 2 * u] = both[:bands]
            terms[slot, 2 * u + 1] = both[bands:]

        tiles(part, at, one)

    def scatter(base, slot):
        for n in range(2 * group):
            term = terms[slot, n]
            for k in range(2):
                sums[k][spots_ref[2 * base + 2 * n + k]] += term

    for part in range(parts):
        products(part, 0, 0)

        def step(n, carry):
            scatter(2 * (part * per_part + (n - 1) * group), (n - 1) % 2)
            products(part, n * group, n % 2)
            return carry

        steps = per_part // group
        lax.fori_loop(1, steps, step, 0)
        scatter(2 * (part * per_part + (steps - 1) * group), (steps - 1) % 2)

    def join(part, at, slot):
        def one(u, p, lanes):
            here = jnp.where(low, first[p], second[p])
            there = jnp.where(low, first[pairs + p], second[pairs + p])
            resid = moved_ref[part, :, lanes].astype(jnp.float32) + here + pltpu.roll(there, half, 1)
            resid_ref[:, pl.ds(pl.multiple_of(p * LANES, LANES), LANES)] = resid
            picked[p] = resid.astype(jnp.bfloat16)
            picked[pairs + p] = pltpu.roll(resid, half, 1).astype(jnp.bfloat16)

        tiles(part, at, one)

    for part in range(parts):
        over(part, join)

    def gather(part, at, slot):
        base = 4 * (part * per_part + at)

        def one(u, p, lanes):
            sources = []
            for q in range(2):
                spot = base + 4 * u + 2 * q
                sources.append(jnp.where(low16, picked[spots_ref[spot]], picked[spots_ref[spot + 1]]))
            both = lax.dot_general(
                jnp.concatenate(sources, axis=0),
                mats_ref[p],
                (((1,), (1,)), ((), ())),
                preferred_element_type=jnp.float32,
            )
            both = jnp.where(low, both[:bands], both[bands:])
            mixed_ref[part, :, lanes] = (picked[p].astype(jnp.float32) + both).astype(jnp.bfloat16)

        tiles(part, at, one)

    for part in range(parts):
        over(part, gather)


def forward_kernel(starts_ref, keys_ref, weight_ref, mixed_ref, pert_ref, vert_ref, field_ref, obs_ref):
    levels, ncols = pert_ref.shape
    members = lax.axis_size("mem")
    wide, chunks, group = grouping(levels, ncols)
    rows = chunks * group
    scale_inv = 1.0 / math.sqrt(members)
    for c in range(chunks):
        part = slice(c * wide, (c + 1) * wide)
        mixed = mixed_ref[:, part]
        localized = mixed.astype(jnp.float32) + jnp.dot(
            vert_ref[...], mixed, preferred_element_type=jnp.float32
        )
        field = (pert_ref[:, part].astype(jnp.float32) * localized * scale_inv).astype(jnp.bfloat16)
        for g in range(levels // group):
            field_ref[g, c * group : (c + 1) * group, :] = field[g * group : (g + 1) * group, :]

    obs_ref[...] = jnp.zeros_like(obs_ref)
    nobs = weight_ref.shape[1]
    ncol = lax.axis_size("col")
    mine = lax.axis_index("col")

    def collect(g, carry):
        runs = runs_of(starts_ref, g, mine, ncol)

        def step(trip, carry):
            spans, rights, hots, rows_of = [], [], [], []
            for run in runs:
                which = run[0]
                span, valid = window_of(run, trip, nobs)
                width = width_of(which)
                lane = keys_ref[2 * which + 1 : 2 * which + 2, span]
                hots.append(one_hot(lane, row_numbers(wide, width), jnp.ones((1, width), jnp.bfloat16)))
                rows_of.append(jnp.where(valid, keys_ref[2 * which : 2 * which + 1, span], -1.0))
                weight = weight_ref[:, span]
                rights.append(1.0 - weight if which else weight)
                spans.append(span)
            hot = jnp.concatenate(hots, axis=1)
            lines = jnp.dot(field_ref[g], hot, preferred_element_type=jnp.float32).astype(jnp.bfloat16)
            at = 0
            for span, right, row in zip(spans, rights, rows_of):
                width = row.shape[1]
                kept = one_hot(row, row_numbers(rows, width), lines[:, at : at + width])
                found = kept[:SUBLANES]
                for r in range(SUBLANES, rows, SUBLANES):
                    found = found + kept[r : r + SUBLANES]
                obs_ref[:, span] += right * jnp.sum(found.astype(jnp.float32), axis=0, keepdims=True)
                at += width
            return carry

        lax.fori_loop(0, trips_of(runs), step, 0)
        return carry

    lax.fori_loop(0, levels // group, collect, 0)


def finish_kernel(*refs, seen, group, wide):
    precision_ref, err_ref, guide_ref, image_ref, norm_ref = refs[:5]
    refs = refs[5:]
    seen_refs, refs = refs[:seen], refs[seen:]
    state_ref, field_ref = refs[-2:]
    refs = refs[:-2]
    steps = len(refs) // 4 + 1
    alphas, betas, rest = refs[: steps - 1], refs[steps - 1 : 2 * steps - 2], refs[2 * steps - 2 :]
    resids, fields = rest[:steps], rest[steps:]
    before = (guide_ref[...], image_ref[...], norm_ref[:, :1])
    alpha, beta, _, _, _ = advance(seen_refs, precision_ref[...], err_ref[...], before)
    alphas = [a[:, :1] for a in alphas] + [alpha]
    betas = [b[:, :1] for b in betas] + [beta]
    mix, shares = [], []
    for a, b in zip(alphas, betas):
        mix = [b * m for m in mix] + [jnp.ones_like(a)]
        shares = [s + a * m for s, m in zip(shares + [jnp.zeros_like(a)], mix)]
    state = shares[0] * resids[0][...]
    for share, resid in zip(shares[1:], resids[1:]):
        state = state + share * resid[...]
    state_ref[...] = state.astype(jnp.bfloat16)
    groups, rows, _ = fields[0].shape
    core = lax.axis_index("mem") % 2
    for g in range(groups):
        total = shares[0] * fields[0][g].astype(jnp.float32)
        for share, field in zip(shares[1:], fields[1:]):
            total = total + share * field[g].astype(jnp.float32)
        total = total.astype(jnp.bfloat16)
        for c in range(rows // group):
            part = slice(c * wide, (c + 1) * wide)
            if len(field_ref.shape) == 2:
                field_ref[g * group : (g + 1) * group, part] = total[c * group : (c + 1) * group, :]
            else:
                size = field_ref.shape[2]
                for s in range(group // size):
                    number = g * (group // size) + s
                    field_ref[(number % 2) ^ core, number // 2, :, part] = total[
                        c * group + s * size : c * group + (s + 1) * size, :
                    ]


def local_call(kernel, outs, args, name, scratch=(), scalars=1, remote=0):
    spaces = [pltpu.SMEM] * scalars + [pltpu.HBM] * remote + [pltpu.VMEM] * (len(args) - scalars - remote)
    kept = [
        a if space is pltpu.SMEM else pltpu.with_memory_space_constraint(a, space)
        for a, space in zip(args, spaces)
    ]
    return pl.pallas_call(
        kernel,
        out_shape=tuple(pltpu.VMEM(o.shape, o.dtype) for o in outs),
        in_specs=[pl.BlockSpec(memory_space=space) for space in spaces],
        out_specs=(pl.BlockSpec(memory_space=pltpu.VMEM),) * len(outs),
        scratch_shapes=list(scratch),
        compiler_params=pltpu.CompilerParams(vmem_limit_bytes=VMEM_BYTES),
        name=name,
    )(*kept)


def swap(x, axis, offset):
    n = lax.axis_size(axis)
    return lax.ppermute(x, axis, [(i, i ^ offset) for i in range(n)])


def total_over(x, axis, offsets):
    return sum([swap(x, axis, k) for k in offsets], x)


def shares_everywhere(x):
    x = total_over(x, "mem", (1,))
    x = total_over(x, "col", range(1, lax.axis_size("col")))
    return [x] + [swap(x, "mem", k) for k in range(2, lax.axis_size("mem"), 2)]


def scatter_members(field):
    if field.ndim == 2:
        nmem = lax.axis_size("mem")
        field = field.reshape(nmem, field.shape[0] // nmem, field.shape[1])
        pieces = lax.all_to_all(field, "mem", 0, 0, tiled=True)
        return jnp.sum(pieces.astype(jnp.float32), axis=0)
    mine = (field[0].astype(jnp.float32) + swap(field[1], "mem", 1).astype(jnp.float32)).astype(jnp.bfloat16)
    chips = mine.shape[0]
    chip = lax.axis_index("mem") // 2
    total = lax.dynamic_index_in_dim(mine, chip, 0, keepdims=False).astype(jnp.float32)
    for k in range(1, chips):
        piece = lax.dynamic_index_in_dim(mine, chip ^ k, 0, keepdims=False)
        total = total + swap(piece, "mem", 2 * k).astype(jnp.float32)
    return total


def per_device(
    perturbations,
    vertical,
    blocks,
    block_scale,
    block_cols,
    obs_level,
    obs_nodes,
    obs_weight,
    obs_value,
    obs_precision,
):
    local_members, levels, ncols = perturbations.shape
    assert local_members == 1
    nblocks, width, depth = blocks.shape
    assert 2 * width == LANES and depth == LANES
    ncol = lax.axis_size("col")
    nmem = lax.axis_size("mem")
    bands = levels // ncol
    pairs = nblocks // 2
    nodes = nblocks * width
    nobs = obs_level.shape[0]
    pert = perturbations[0]
    wide, chunks, group = grouping(levels, ncols)
    rows = chunks * group
    slices = levels // nmem

    level, node, other = obs_level, obs_nodes[:, 0], obs_nodes[:, 1]
    kind = ((level // group) * ncol + node // ncols) * ncol + other // ncols
    bounds = jnp.arange(levels // group * ncol * ncol + 1, dtype=jnp.int32)
    starts = jnp.sum((kind[None, :] < bounds[:, None]).astype(jnp.int32), axis=1)
    order = (kind * group + level % group) * ncols + node % ncols
    order, other, weight, value, precision = lax.sort(
        (order, other % ncols, obs_weight, obs_value, obs_precision), num_keys=1, is_stable=False
    )
    level = (order // ncols) % group
    keys = []
    for local in (order % ncols, other):
        keys += [(local // wide) * group + level, local % wide]
    keys = jnp.stack(keys).astype(jnp.float32)
    weight, value, precision = (a.reshape(1, nobs) for a in (weight, value, precision))

    tiles = min(TILES, ncols // LANES)
    scales = jnp.repeat(block_scale, width, axis=1)[:, None, :]
    mats = (blocks.astype(jnp.float32) * scales).astype(jnp.bfloat16).reshape(pairs, LANES, depth)
    which = jnp.arange(block_cols.shape[1], dtype=jnp.int32)[None, :]
    spots = (((block_cols & 1) ^ which) * pairs + (block_cols >> 1)).reshape(-1)

    vector = jax.ShapeDtypeStruct((1, nobs), jnp.float32)
    number = jax.ShapeDtypeStruct((1, LANES), jnp.float32)
    moved_shape = jax.ShapeDtypeStruct((ncol, bands, ncols), jnp.bfloat16)

    def adjoint(errors, seen, before):
        count = len(seen)
        outs = (moved_shape, vector) + ((number, number, vector, vector, number) if count else ())
        extra = (list(before) if before is not None else []) + list(seen)
        return local_call(
            functools.partial(adjoint_kernel, seen=count, first=before is None),
            outs,
            [starts, pert, vertical, keys, weight, precision, errors, *extra],
            "adjoint",
            [
                pltpu.VMEM((rows, wide), jnp.float32),
                pltpu.VMEM((levels, ncols), jnp.float32),
                pltpu.VMEM((levels, ncols), jnp.bfloat16),
                pltpu.VMEM((levels, levels), jnp.bfloat16),
                pltpu.SemaphoreType.DMA((2,)),
            ],
            remote=2,
        )

    def middle(moved):
        vmem = pl.BlockSpec(memory_space=pltpu.VMEM)
        return pl.pallas_call(
            horizontal_kernel,
            out_shape=(
                pltpu.VMEM((bands, nodes), jnp.float32),
                pltpu.VMEM(moved_shape.shape, moved_shape.dtype),
            ),
            in_specs=[pl.BlockSpec(memory_space=pltpu.SMEM), vmem, vmem],
            out_specs=(vmem, vmem),
            scratch_shapes=[
                pltpu.VMEM((2, 2 * tiles, bands, LANES), jnp.float32),
                pltpu.VMEM((2 * pairs, bands, LANES), jnp.float32),
                pltpu.VMEM((2 * pairs, bands, LANES), jnp.float32),
                pltpu.VMEM((2 * pairs, bands, LANES), jnp.bfloat16),
            ],
            compiler_params=pltpu.CompilerParams(vmem_limit_bytes=VMEM_BYTES),
            name="horizontal",
        )(
            spots,
            pltpu.with_memory_space_constraint(moved, pltpu.VMEM),
            pltpu.with_memory_space_constraint(mats, pltpu.VMEM),
        )

    def forward(columns):
        field = jax.ShapeDtypeStruct((levels // group, rows, wide), jnp.bfloat16)
        return local_call(
            forward_kernel, (field, vector), [starts, keys, weight, columns, pert, vertical], "forward"
        )

    errors, seen, before = value, (), None
    alphas, betas, fields, resids = [], [], [], []
    for step in range(ITERS):
        if step == 0:
            sent, errors = adjoint(errors, seen, None)
        else:
            sent, errors, alpha, beta, *before = adjoint(errors, seen, before)
            alphas.append(alpha)
            betas.append(beta)
        moved = lax.all_to_all(sent, "col", 0, 0, tiled=True)
        resid, mixed = middle(moved)
        columns = lax.all_to_all(mixed, "col", 0, 0, tiled=True).reshape(levels, ncols)
        field, partial = forward(columns)
        seen = shares_everywhere(partial)
        resids.append(resid)
        fields.append(field)

    split = slices % 16 == 0 and group % slices == 0
    field_shape = (2, nmem // 2, slices, ncols) if split else (levels, ncols)
    args = [precision, errors, *before, *seen, *alphas, *betas, *resids, *fields]
    state, total = local_call(
        functools.partial(finish_kernel, seen=len(seen), group=group, wide=wide),
        (
            jax.ShapeDtypeStruct((bands, nodes), jnp.bfloat16),
            jax.ShapeDtypeStruct(field_shape, jnp.bfloat16),
        ),
        args,
        "finish",
        scalars=0,
    )
    return (state[None], scatter_members(total))


def solution(mesh):
    in_specs = (P("mem", None, "col"), P(), P(), P(), P(), P(), P(), P(), P(), P())
    out_specs = (P("mem", "col", None), P("mem", "col"))
    return jax.shard_map(
        per_device, mesh=mesh, in_specs=in_specs, out_specs=out_specs, check_vma=False
    )
```

```python
import functools
import math

import jax
import jax.numpy as jnp
from jax import lax
from jax.experimental import pallas as pl
from jax.experimental.pallas import tpu as pltpu
from jax.sharding import PartitionSpec as P

ITERS = 2
LANES = 128
SUBLANES = 16
WIDE = 256
ROWS = 256
FIRST = 768
SECOND = 384
TILES = 8
VMEM_BYTES = 24 << 20


def grouping(levels, ncols):
    wide = min(WIDE, ncols)
    chunks = ncols // wide
    group = max(8, min(levels, ROWS // chunks))
    return wide, chunks, group


def one_hot(keys, numbers, values):
    key = jnp.broadcast_to(keys.astype(jnp.bfloat16), numbers.shape)
    val = jnp.broadcast_to(values, numbers.shape)
    return jnp.where(numbers == key, val, jnp.zeros_like(val))


def row_numbers(rows, n):
    return lax.broadcasted_iota(jnp.int32, (rows, n), 0).astype(jnp.float32).astype(jnp.bfloat16)


def runs_of(starts_ref, g, mine, ncol):
    runs = [(0, starts_ref[(g * ncol + mine) * ncol], starts_ref[(g * ncol + mine + 1) * ncol])]
    for other in range(ncol):
        at = (g * ncol + other) * ncol + mine
        runs.append((1, starts_ref[at], starts_ref[at + 1]))
    return runs


def width_of(which):
    return SECOND if which else FIRST


def trips_of(runs):
    trips = jnp.int32(0)
    for which, low, end in runs:
        need = (end - (low // LANES) * LANES + width_of(which) - 1) // width_of(which)
        trips = jnp.maximum(trips, jnp.where(end > low, need, 0))
    return trips


def window_of(run, trip, nobs):
    which, low, end = run
    width = width_of(which)
    first = (low // LANES) * LANES + trip * width
    base = pl.multiple_of(jnp.minimum(first, nobs - width), LANES)
    place = base + lax.broadcasted_iota(jnp.int32, (1, width), 1)
    valid = (place >= jnp.maximum(low, first)) & (place < jnp.minimum(end, first + width))
    return pl.ds(base, width), valid


def total_of(x):
    return jnp.sum(x, axis=1, keepdims=True)


def advance(seen_refs, precision, errors, previous):
    seen = seen_refs[0][...]
    for ref in seen_refs[1:]:
        seen = seen + ref[...]
    norm = total_of(errors * seen)
    if previous is None:
        beta = jnp.zeros_like(norm)
        guide, image = errors, seen
    else:
        beta = norm / previous[2]
        guide, image = errors + beta * previous[0], seen + beta * previous[1]
    along = total_of(guide * image) + total_of(precision * image * image)
    return norm / along, beta, guide, image, norm


def adjoint_kernel(*refs, seen, first):
    starts_ref, pert_hbm, vert_hbm, keys_ref, weight_ref, precision_ref, err_ref = refs[:7]
    pert_ref, vert_ref, sems = refs[-3:]
    refs = refs[7:-3]
    levels, ncols = pert_ref.shape
    copies = [
        pltpu.make_async_copy(pert_hbm, pert_ref, sems.at[0]),
        pltpu.make_async_copy(vert_hbm, vert_ref, sems.at[1]),
    ]
    for copy in copies:
        copy.start()
    members = lax.axis_size("mem")
    wide, chunks, group = grouping(levels, ncols)
    rows = chunks * group
    if seen:
        before, refs = (None, refs) if first else ([r[...] for r in refs[:3]], refs[3:])
        seen_refs, refs = refs[:seen], refs[seen:]
        out_ref, new_ref, alpha_ref, beta_ref, guide_ref, image_ref, norm_ref, total, field = refs
        if before is not None:
            before[2] = before[2][:, :1]
        errors, precision = err_ref[...], precision_ref[...]
        alpha, beta, guide, image, norm = advance(seen_refs, precision, errors, before)
        new_ref[...] = errors - alpha * (guide + precision * image)
        guide_ref[...] = guide
        image_ref[...] = image
        for ref, value in ((alpha_ref, alpha), (beta_ref, beta), (norm_ref, norm)):
            ref[...] = jnp.broadcast_to(value, ref.shape)
    else:
        out_ref, new_ref, total, field = refs
        new_ref[...] = precision_ref[...] * err_ref[...]
    bands = out_ref.shape[1]
    nobs = weight_ref.shape[1]
    ncol = lax.axis_size("col")
    mine = lax.axis_index("col")

    def collect(g, carry):
        total[...] = jnp.zeros_like(total)
        runs = runs_of(starts_ref, g, mine, ncol)

        def step(trip, carry):
            above, beside = [], []
            for run in runs:
                which = run[0]
                span, valid = window_of(run, trip, nobs)
                weight = weight_ref[:, span]
                weight = 1.0 - weight if which else weight
                row = jnp.where(valid, keys_ref[2 * which : 2 * which + 1, span], -1.0)
                lane = keys_ref[2 * which + 1 : 2 * which + 2, span]
                width = width_of(which)
                above.append(one_hot(row, row_numbers(rows, width), (weight * new_ref[:, span]).astype(jnp.bfloat16)))
                beside.append(one_hot(lane, row_numbers(wide, width), jnp.ones((1, width), jnp.bfloat16)))
            total[...] += lax.dot_general(
                jnp.concatenate(above, axis=1),
                jnp.concatenate(beside, axis=1),
                (((1,), (1,)), ((), ())),
                preferred_element_type=jnp.float32,
            )
            return carry

        lax.fori_loop(0, trips_of(runs), step, 0)
        here = pl.ds(pl.multiple_of(g * group, group), group)
        for c in range(chunks):
            field[here, c * wide : (c + 1) * wide] = total[c * group : (c + 1) * group, :]
        return carry

    lax.fori_loop(0, levels // group, collect, 0)

    for copy in copies:
        copy.wait()
    scale_inv = 1.0 / math.sqrt(members)
    for c in range(chunks):
        part = slice(c * wide, (c + 1) * wide)
        scaled = (pert_ref[:, part].astype(jnp.float32) * field[:, part] * scale_inv).astype(jnp.bfloat16)
        turned = scaled.astype(jnp.float32) + lax.dot_general(
            vert_ref[...], scaled, (((0,), (0,)), ((), ())), preferred_element_type=jnp.float32
        )
        for b in range(out_ref.shape[0]):
            out_ref[b, :, part] = turned[b * bands : (b + 1) * bands, :].astype(jnp.bfloat16)


def horizontal_kernel(
    spots_ref, scale_ref, moved_ref, mats_ref, resid_ref, mixed_ref, terms, first, second, picked
):
    parts, bands, ncols = moved_ref.shape
    pairs = mats_ref.shape[0]
    per_part = ncols // LANES
    group = terms.shape[1] // 2
    half = LANES // 2
    lane = lax.broadcasted_iota(jnp.int32, (bands, LANES), 1)
    low = lane < half
    low16 = lane.astype(jnp.float32).astype(jnp.bfloat16) < half
    sums = (first, second)

    for s in sums:
        s[...] = jnp.zeros_like(s)

    def tiles(part, at, body):
        for u in range(group):
            lanes = pl.ds(pl.multiple_of((at + u) * LANES, LANES), LANES)
            body(u, part * per_part + at + u, lanes)

    def over(part, function):
        lax.fori_loop(0, per_part // group, lambda n, c: function(part, n * group, n % 2) or c, 0)

    def products(part, at, slot):
        def one(u, p, lanes):
            tile = moved_ref[part, :, lanes]
            none = jnp.zeros_like(tile)
            tall = jnp.concatenate([jnp.where(low16, tile, none), jnp.where(low16, none, tile)], axis=0)
            both = jnp.dot(tall, mats_ref[p], preferred_element_type=jnp.float32)
            for q in range(2):
                scale = jnp.where(low[:1], scale_ref[0, 2 * p + q], scale_ref[1, 2 * p + q])
                terms[slot, 2 * u + q] = both[q * bands : (q + 1) * bands] * scale

        tiles(part, at, one)

    def scatter(base, slot):
        for n in range(2 * group):
            term = terms[slot, n]
            for k in range(2):
                sums[k][spots_ref[2 * base + 2 * n + k]] += term

    for part in range(parts):
        products(part, 0, 0)

        def step(n, carry):
            scatter(2 * (part * per_part + (n - 1) * group), (n - 1) % 2)
            products(part, n * group, n % 2)
            return carry

        steps = per_part // group
        lax.fori_loop(1, steps, step, 0)
        scatter(2 * (part * per_part + (steps - 1) * group), (steps - 1) % 2)

    def join(part, at, slot):
        def one(u, p, lanes):
            here = jnp.where(low, first[p], second[p])
            there = jnp.where(low, first[pairs + p], second[pairs + p])
            resid = moved_ref[part, :, lanes].astype(jnp.float32) + here + pltpu.roll(there, half, 1)
            resid_ref[:, pl.ds(pl.multiple_of(p * LANES, LANES), LANES)] = resid
            picked[p] = resid.astype(jnp.bfloat16)
            picked[pairs + p] = pltpu.roll(resid, half, 1).astype(jnp.bfloat16)

        tiles(part, at, one)

    for part in range(parts):
        over(part, join)

    def gather(part, at, slot):
        base = 4 * (part * per_part + at)

        def one(u, p, lanes):
            sources = []
            for q in range(2):
                spot = base + 4 * u + 2 * q
                one, two = picked[spots_ref[spot]], picked[spots_ref[spot + 1]]
                none = jnp.zeros_like(one)
                sources += [jnp.where(low16, one, none), jnp.where(low16, none, two)]
            each = lax.dot_general(
                jnp.concatenate(sources, axis=0),
                mats_ref[p],
                (((1,), (1,)), ((), ())),
                preferred_element_type=jnp.float32,
            )
            halves = [
                scale_ref[0, 2 * p + q] * each[2 * q * bands : (2 * q + 1) * bands]
                + scale_ref[1, 2 * p + q] * each[(2 * q + 1) * bands : (2 * q + 2) * bands]
                for q in range(2)
            ]
            both = jnp.where(low, halves[0], halves[1])
            mixed_ref[part, :, lanes] = (picked[p].astype(jnp.float32) + both).astype(jnp.bfloat16)

        tiles(part, at, one)

    for part in range(parts):
        over(part, gather)


def forward_kernel(starts_ref, keys_ref, weight_ref, mixed_ref, pert_ref, vert_ref, field_ref, obs_ref):
    levels, ncols = pert_ref.shape
    members = lax.axis_size("mem")
    wide, chunks, group = grouping(levels, ncols)
    rows = chunks * group
    scale_inv = 1.0 / math.sqrt(members)
    for c in range(chunks):
        part = slice(c * wide, (c + 1) * wide)
        mixed = mixed_ref[:, part]
        localized = mixed.astype(jnp.float32) + jnp.dot(
            vert_ref[...], mixed, preferred_element_type=jnp.float32
        )
        field = (pert_ref[:, part].astype(jnp.float32) * localized * scale_inv).astype(jnp.bfloat16)
        for g in range(levels // group):
            field_ref[g, c * group : (c + 1) * group, :] = field[g * group : (g + 1) * group, :]

    obs_ref[...] = jnp.zeros_like(obs_ref)
    nobs = weight_ref.shape[1]
    ncol = lax.axis_size("col")
    mine = lax.axis_index("col")

    def collect(g, carry):
        runs = runs_of(starts_ref, g, mine, ncol)

        def step(trip, carry):
            spans, rights, hots, rows_of = [], [], [], []
            for run in runs:
                which = run[0]
                span, valid = window_of(run, trip, nobs)
                width = width_of(which)
                lane = keys_ref[2 * which + 1 : 2 * which + 2, span]
                hots.append(one_hot(lane, row_numbers(wide, width), jnp.ones((1, width), jnp.bfloat16)))
                rows_of.append(jnp.where(valid, keys_ref[2 * which : 2 * which + 1, span], -1.0))
                weight = weight_ref[:, span]
                rights.append(1.0 - weight if which else weight)
                spans.append(span)
            hot = jnp.concatenate(hots, axis=1)
            lines = jnp.dot(field_ref[g], hot, preferred_element_type=jnp.float32).astype(jnp.bfloat16)
            at = 0
            for span, right, row in zip(spans, rights, rows_of):
                width = row.shape[1]
                kept = one_hot(row, row_numbers(rows, width), lines[:, at : at + width])
                found = kept[:SUBLANES]
                for r in range(SUBLANES, rows, SUBLANES):
                    found = found + kept[r : r + SUBLANES]
                obs_ref[:, span] += right * jnp.sum(found.astype(jnp.float32), axis=0, keepdims=True)
                at += width
            return carry

        lax.fori_loop(0, trips_of(runs), step, 0)
        return carry

    lax.fori_loop(0, levels // group, collect, 0)


def finish_kernel(*refs, seen, group, wide):
    precision_ref, err_ref, guide_ref, image_ref, norm_ref = refs[:5]
    refs = refs[5:]
    seen_refs, refs = refs[:seen], refs[seen:]
    state_ref, field_ref = refs[-2:]
    refs = refs[:-2]
    steps = len(refs) // 4 + 1
    alphas, betas, rest = refs[: steps - 1], refs[steps - 1 : 2 * steps - 2], refs[2 * steps - 2 :]
    resids, fields = rest[:steps], rest[steps:]
    before = (guide_ref[...], image_ref[...], norm_ref[:, :1])
    alpha, beta, _, _, _ = advance(seen_refs, precision_ref[...], err_ref[...], before)
    alphas = [a[:, :1] for a in alphas] + [alpha]
    betas = [b[:, :1] for b in betas] + [beta]
    mix, shares = [], []
    for a, b in zip(alphas, betas):
        mix = [b * m for m in mix] + [jnp.ones_like(a)]
        shares = [s + a * m for s, m in zip(shares + [jnp.zeros_like(a)], mix)]
    state = shares[0] * resids[0][...]
    for share, resid in zip(shares[1:], resids[1:]):
        state = state + share * resid[...]
    state_ref[...] = state.astype(jnp.bfloat16)
    groups, rows, _ = fields[0].shape
    core = lax.axis_index("mem") % 2
    for g in range(groups):
        total = shares[0] * fields[0][g].astype(jnp.float32)
        for share, field in zip(shares[1:], fields[1:]):
            total = total + share * field[g].astype(jnp.float32)
        total = total.astype(jnp.bfloat16)
        for c in range(rows // group):
            part = slice(c * wide, (c + 1) * wide)
            if len(field_ref.shape) == 2:
                field_ref[g * group : (g + 1) * group, part] = total[c * group : (c + 1) * group, :]
            else:
                size = field_ref.shape[2]
                for s in range(group // size):
                    number = g * (group // size) + s
                    field_ref[(number % 2) ^ core, number // 2, :, part] = total[
                        c * group + s * size : c * group + (s + 1) * size, :
                    ]


def local_call(kernel, outs, args, name, scratch=(), scalars=1, remote=0):
    spaces = [pltpu.SMEM] * scalars + [pltpu.HBM] * remote + [pltpu.VMEM] * (len(args) - scalars - remote)
    kept = [
        a if space is pltpu.SMEM else pltpu.with_memory_space_constraint(a, space)
        for a, space in zip(args, spaces)
    ]
    return pl.pallas_call(
        kernel,
        out_shape=tuple(pltpu.VMEM(o.shape, o.dtype) for o in outs),
        in_specs=[pl.BlockSpec(memory_space=space) for space in spaces],
        out_specs=(pl.BlockSpec(memory_space=pltpu.VMEM),) * len(outs),
        scratch_shapes=list(scratch),
        compiler_params=pltpu.CompilerParams(vmem_limit_bytes=VMEM_BYTES),
        name=name,
    )(*kept)


def swap(x, axis, offset):
    n = lax.axis_size(axis)
    return lax.ppermute(x, axis, [(i, i ^ offset) for i in range(n)])


def total_over(x, axis, offsets):
    return sum([swap(x, axis, k) for k in offsets], x)


def shares_everywhere(x):
    shape = x.shape
    x = x.reshape(-1, LANES)
    x = total_over(x, "mem", (1,))
    x = total_over(x, "mem", range(2, lax.axis_size("mem"), 2))
    return [y.reshape(shape) for y in [x] + [swap(x, "col", k) for k in range(1, lax.axis_size("col"))]]


def scatter_members(field):
    if field.ndim == 2:
        nmem = lax.axis_size("mem")
        field = field.reshape(nmem, field.shape[0] // nmem, field.shape[1])
        pieces = lax.all_to_all(field, "mem", 0, 0, tiled=True)
        return jnp.sum(pieces.astype(jnp.float32), axis=0)
    mine = (field[0].astype(jnp.float32) + swap(field[1], "mem", 1).astype(jnp.float32)).astype(jnp.bfloat16)
    chips = mine.shape[0]
    chip = lax.axis_index("mem") // 2
    total = lax.dynamic_index_in_dim(mine, chip, 0, keepdims=False).astype(jnp.float32)
    for k in range(1, chips):
        piece = lax.dynamic_index_in_dim(mine, chip ^ k, 0, keepdims=False)
        total = total + swap(piece, "mem", 2 * k).astype(jnp.float32)
    return total


def per_device(
    perturbations,
    vertical,
    blocks,
    block_scale,
    block_cols,
    obs_level,
    obs_nodes,
    obs_weight,
    obs_value,
    obs_precision,
):
    local_members, levels, ncols = perturbations.shape
    assert local_members == 1
    nblocks, width, depth = blocks.shape
    assert 2 * width == LANES and depth == LANES
    ncol = lax.axis_size("col")
    nmem = lax.axis_size("mem")
    bands = levels // ncol
    pairs = nblocks // 2
    nodes = nblocks * width
    nobs = obs_level.shape[0]
    pert = perturbations[0]
    wide, chunks, group = grouping(levels, ncols)
    rows = chunks * group
    slices = levels // nmem

    level, node, other = obs_level, obs_nodes[:, 0], obs_nodes[:, 1]
    kind = ((level // group) * ncol + node // ncols) * ncol + other // ncols
    bounds = jnp.arange(levels // group * ncol * ncol + 1, dtype=jnp.int32)
    starts = jnp.sum((kind[None, :] < bounds[:, None]).astype(jnp.int32), axis=1)
    order = (kind * group + level % group) * ncols + node % ncols
    order, other, weight, value, precision = lax.sort(
        (order, other % ncols, obs_weight, obs_value, obs_precision), num_keys=1, is_stable=False
    )
    level = (order // ncols) % group
    keys = []
    for local in (order % ncols, other):
        keys += [(local // wide) * group + level, local % wide]
    keys = jnp.stack(keys).astype(jnp.float32)
    weight, value, precision = (a.reshape(1, nobs) for a in (weight, value, precision))

    tiles = min(TILES, ncols // LANES)
    mats = blocks.reshape(pairs, LANES, depth)
    which = jnp.arange(block_cols.shape[1], dtype=jnp.int32)[None, :]
    spots = (((block_cols & 1) ^ which) * pairs + (block_cols >> 1)).reshape(-1)

    vector = jax.ShapeDtypeStruct((1, nobs), jnp.float32)
    number = jax.ShapeDtypeStruct((1, LANES), jnp.float32)
    moved_shape = jax.ShapeDtypeStruct((ncol, bands, ncols), jnp.bfloat16)

    def adjoint(errors, seen, before):
        count = len(seen)
        outs = (moved_shape, vector) + ((number, number, vector, vector, number) if count else ())
        extra = (list(before) if before is not None else []) + list(seen)
        return local_call(
            functools.partial(adjoint_kernel, seen=count, first=before is None),
            outs,
            [starts, pert, vertical, keys, weight, precision, errors, *extra],
            "adjoint",
            [
                pltpu.VMEM((rows, wide), jnp.float32),
                pltpu.VMEM((levels, ncols), jnp.float32),
                pltpu.VMEM((levels, ncols), jnp.bfloat16),
                pltpu.VMEM((levels, levels), jnp.bfloat16),
                pltpu.SemaphoreType.DMA((2,)),
            ],
            remote=2,
        )

    def middle(moved):
        vmem = pl.BlockSpec(memory_space=pltpu.VMEM)
        smem = pl.BlockSpec(memory_space=pltpu.SMEM)
        return pl.pallas_call(
            horizontal_kernel,
            out_shape=(
                pltpu.VMEM((bands, nodes), jnp.float32),
                pltpu.VMEM(moved_shape.shape, moved_shape.dtype),
            ),
            in_specs=[smem, smem, vmem, vmem],
            out_specs=(vmem, vmem),
            scratch_shapes=[
                pltpu.VMEM((2, 2 * tiles, bands, LANES), jnp.float32),
                pltpu.VMEM((2 * pairs, bands, LANES), jnp.float32),
                pltpu.VMEM((2 * pairs, bands, LANES), jnp.float32),
                pltpu.VMEM((2 * pairs, bands, LANES), jnp.bfloat16),
            ],
            compiler_params=pltpu.CompilerParams(vmem_limit_bytes=VMEM_BYTES),
            name="horizontal",
        )(
            spots,
            block_scale.T,
            pltpu.with_memory_space_constraint(moved, pltpu.VMEM),
            pltpu.with_memory_space_constraint(mats, pltpu.VMEM),
        )

    def forward(columns):
        field = jax.ShapeDtypeStruct((levels // group, rows, wide), jnp.bfloat16)
        return local_call(
            forward_kernel, (field, vector), [starts, keys, weight, columns, pert, vertical], "forward"
        )

    errors, seen, before = value, (), None
    alphas, betas, fields, resids = [], [], [], []
    for step in range(ITERS):
        if step == 0:
            sent, errors = adjoint(errors, seen, None)
        else:
            sent, errors, alpha, beta, *before = adjoint(errors, seen, before)
            alphas.append(alpha)
            betas.append(beta)
        moved = lax.all_to_all(sent, "col", 0, 0, tiled=True)
        resid, mixed = middle(moved)
        columns = lax.all_to_all(mixed, "col", 0, 0, tiled=True).reshape(levels, ncols)
        field, partial = forward(columns)
        seen = shares_everywhere(partial)
        resids.append(resid)
        fields.append(field)

    split = slices % 16 == 0 and group % slices == 0
    field_shape = (2, nmem // 2, slices, ncols) if split else (levels, ncols)
    args = [precision, errors, *before, *seen, *alphas, *betas, *resids, *fields]
    state, total = local_call(
        functools.partial(finish_kernel, seen=len(seen), group=group, wide=wide),
        (
            jax.ShapeDtypeStruct((bands, nodes), jnp.bfloat16),
            jax.ShapeDtypeStruct(field_shape, jnp.bfloat16),
        ),
        args,
        "finish",
        scalars=0,
    )
    return (state[None], scatter_members(total))


def solution(mesh):
    in_specs = (P("mem", None, "col"), P(), P(), P(), P(), P(), P(), P(), P(), P())
    out_specs = (P("mem", "col", None), P("mem", "col"))
    return jax.shard_map(
        per_device, mesh=mesh, in_specs=in_specs, out_specs=out_specs, check_vma=False
    )
```

```python
import functools
import math

import jax
import jax.numpy as jnp
from jax import lax
from jax.experimental import pallas as pl
from jax.experimental.pallas import tpu as pltpu
from jax.sharding import PartitionSpec as P

ITERS = 2
LANES = 128
SUBLANES = 16
WIDE = 256
ROWS = 256
FIRST = 768
SECOND = 384
TILES = 16
VMEM_BYTES = 24 << 20


def grouping(levels, ncols):
    wide = min(WIDE, ncols)
    chunks = ncols // wide
    group = max(8, min(levels, ROWS // chunks))
    return wide, chunks, group


def one_hot(keys, numbers, values):
    key = jnp.broadcast_to(keys.astype(jnp.bfloat16), numbers.shape)
    val = jnp.broadcast_to(values, numbers.shape)
    return jnp.where(numbers == key, val, jnp.zeros_like(val))


def row_numbers(rows, n):
    return lax.broadcasted_iota(jnp.int32, (rows, n), 0).astype(jnp.float32).astype(jnp.bfloat16)


def runs_of(starts_ref, g, mine, ncol):
    runs = [(0, starts_ref[(g * ncol + mine) * ncol], starts_ref[(g * ncol + mine + 1) * ncol])]
    for other in range(ncol):
        at = (g * ncol + other) * ncol + mine
        runs.append((1, starts_ref[at], starts_ref[at + 1]))
    return runs


def width_of(which):
    return SECOND if which else FIRST


def trips_of(runs):
    trips = jnp.int32(0)
    for which, low, end in runs:
        need = (end - (low // LANES) * LANES + width_of(which) - 1) // width_of(which)
        trips = jnp.maximum(trips, jnp.where(end > low, need, 0))
    return trips


def window_of(run, trip, nobs):
    which, low, end = run
    width = width_of(which)
    first = (low // LANES) * LANES + trip * width
    base = pl.multiple_of(jnp.minimum(first, nobs - width), LANES)
    place = base + lax.broadcasted_iota(jnp.int32, (1, width), 1)
    valid = (place >= jnp.maximum(low, first)) & (place < jnp.minimum(end, first + width))
    return pl.ds(base, width), valid


def total_of(x):
    return jnp.sum(x, axis=1, keepdims=True)


def advance(seen_refs, precision, errors, previous):
    seen = seen_refs[0][...].astype(jnp.float32)
    for ref in seen_refs[1:]:
        seen = seen + ref[...].astype(jnp.float32)
    norm = total_of(errors * seen)
    if previous is None:
        beta = jnp.zeros_like(norm)
        guide, image = errors, seen
    else:
        beta = norm / previous[2]
        guide, image = errors + beta * previous[0], seen + beta * previous[1]
    along = total_of(guide * image) + total_of(precision * image * image)
    return norm / along, beta, guide, image, norm


def adjoint_kernel(*refs, seen, first):
    starts_ref, pert_hbm, vert_hbm, keys_ref, weight_ref, precision_ref, err_ref = refs[:7]
    pert_ref, vert_ref, sems = refs[-3:]
    refs = refs[7:-3]
    levels, ncols = pert_ref.shape
    copies = [
        pltpu.make_async_copy(pert_hbm, pert_ref, sems.at[0]),
        pltpu.make_async_copy(vert_hbm, vert_ref, sems.at[1]),
    ]
    for copy in copies:
        copy.start()
    members = lax.axis_size("mem")
    wide, chunks, group = grouping(levels, ncols)
    rows = chunks * group
    if seen:
        before, refs = (None, refs) if first else ([r[...] for r in refs[:3]], refs[3:])
        seen_refs, refs = refs[:seen], refs[seen:]
        out_ref, new_ref, alpha_ref, beta_ref, guide_ref, image_ref, norm_ref, field = refs
        if before is not None:
            before[2] = before[2][:, :1]
        errors, precision = err_ref[...], precision_ref[...]
        alpha, beta, guide, image, norm = advance(seen_refs, precision, errors, before)
        new_ref[...] = errors - alpha * (guide + precision * image)
        guide_ref[...] = guide
        image_ref[...] = image
        for ref, value in ((alpha_ref, alpha), (beta_ref, beta), (norm_ref, norm)):
            ref[...] = jnp.broadcast_to(value, ref.shape)
    else:
        out_ref, new_ref, field = refs
        new_ref[...] = precision_ref[...] * err_ref[...]
    bands = out_ref.shape[1]
    nobs = weight_ref.shape[1]
    ncol = lax.axis_size("col")
    mine = lax.axis_index("col")

    def product(g, trip):
        above, beside = [], []
        for run in runs_of(starts_ref, g, mine, ncol):
            which = run[0]
            span, valid = window_of(run, trip, nobs)
            weight = weight_ref[:, span]
            weight = 1.0 - weight if which else weight
            row = jnp.where(valid, keys_ref[2 * which : 2 * which + 1, span], -1.0)
            lane = keys_ref[2 * which + 1 : 2 * which + 2, span]
            width = width_of(which)
            above.append(one_hot(row, row_numbers(rows, width), (weight * new_ref[:, span]).astype(jnp.bfloat16)))
            beside.append(one_hot(lane, row_numbers(wide, width), jnp.ones((1, width), jnp.bfloat16)))
        return lax.dot_general(
            jnp.concatenate(above, axis=1),
            jnp.concatenate(beside, axis=1),
            (((1,), (1,)), ((), ())),
            preferred_element_type=jnp.float32,
        )

    for g in range(levels // group):
        result = product(g, 0)
        for c in range(chunks):
            field[g * group : (g + 1) * group, c * wide : (c + 1) * wide] = result[c * group : (c + 1) * group]

    def collect(g, carry):
        here = pl.ds(pl.multiple_of(g * group, group), group)

        def step(trip, carry):
            result = product(g, trip)
            for c in range(chunks):
                field[here, c * wide : (c + 1) * wide] += result[c * group : (c + 1) * group]
            return carry

        return lax.fori_loop(1, trips_of(runs_of(starts_ref, g, mine, ncol)), step, carry)

    lax.fori_loop(0, levels // group, collect, 0)
    for copy in copies:
        copy.wait()
    scale_inv = 1.0 / math.sqrt(members)
    for c in range(chunks):
        part = slice(c * wide, (c + 1) * wide)
        scaled = (pert_ref[:, part].astype(jnp.float32) * field[:, part] * scale_inv).astype(jnp.bfloat16)
        turned = scaled.astype(jnp.float32) + lax.dot_general(
            vert_ref[...], scaled, (((0,), (0,)), ((), ())), preferred_element_type=jnp.float32
        )
        for b in range(out_ref.shape[0]):
            out_ref[b, :, part] = turned[b * bands : (b + 1) * bands, :].astype(jnp.bfloat16)


def horizontal_kernel(
    spots_ref, scale_ref, moved_ref, mats_ref, resid_ref, mixed_ref, terms, first, second, picked
):
    parts, bands, ncols = moved_ref.shape
    pairs = mats_ref.shape[0]
    per_part = ncols // LANES
    group = terms.shape[1] // 2
    half = LANES // 2
    lane = lax.broadcasted_iota(jnp.int32, (bands, LANES), 1)
    low = lane < half
    low16 = lane.astype(jnp.float32).astype(jnp.bfloat16) < half
    sums = (first, second)

    for s in sums:
        s[...] = jnp.zeros_like(s)

    def tiles(part, at, body):
        for u in range(group):
            lanes = pl.ds(pl.multiple_of((at + u) * LANES, LANES), LANES)
            body(u, part * per_part + at + u, lanes)

    def over(part, function):
        if per_part == group:
            function(part, 0, 0)
        else:
            lax.fori_loop(0, per_part // group, lambda n, c: function(part, n * group, n % 2) or c, 0)

    def products(part, at, slot):
        def one(u, p, lanes):
            tile = moved_ref[part, :, lanes]
            none = jnp.zeros_like(tile)
            tall = jnp.concatenate([jnp.where(low16, tile, none), jnp.where(low16, none, tile)], axis=0)
            both = jnp.dot(tall, mats_ref[p], preferred_element_type=jnp.float32)
            for q in range(2):
                scale = jnp.where(low[:1], scale_ref[0, 2 * p + q], scale_ref[1, 2 * p + q])
                terms[slot, 2 * u + q] = both[q * bands : (q + 1) * bands] * scale

        tiles(part, at, one)

    def scatter(base, slot):
        for n in range(2 * group):
            term = terms[slot, n]
            for k in range(2):
                sums[k][spots_ref[2 * base + 2 * n + k]] += term

    steps = per_part // group
    for part in range(parts):
        if steps == 1:
            products(part, 0, part % 2)
            if part > 0:
                scatter(2 * (part - 1) * per_part, (part - 1) % 2)
            continue
        products(part, 0, 0)

        def step(n, carry):
            scatter(2 * (part * per_part + (n - 1) * group), (n - 1) % 2)
            products(part, n * group, n % 2)
            return carry

        lax.fori_loop(1, steps, step, 0)
        scatter(2 * (part * per_part + (steps - 1) * group), (steps - 1) % 2)
    if steps == 1:
        scatter(2 * (parts - 1) * per_part, (parts - 1) % 2)

    def join(part, at, slot):
        def one(u, p, lanes):
            here = jnp.where(low, first[p], second[p])
            there = jnp.where(low, first[pairs + p], second[pairs + p])
            resid = moved_ref[part, :, lanes].astype(jnp.float32) + here + pltpu.roll(there, half, 1)
            resid_ref[:, pl.ds(pl.multiple_of(p * LANES, LANES), LANES)] = resid
            picked[p] = resid.astype(jnp.bfloat16)
            picked[pairs + p] = pltpu.roll(resid, half, 1).astype(jnp.bfloat16)

        tiles(part, at, one)

    for part in range(parts):
        over(part, join)

    def gather(part, at, slot):
        base = 4 * (part * per_part + at)

        def one(u, p, lanes):
            sources = []
            for q in range(2):
                spot = base + 4 * u + 2 * q
                one, two = picked[spots_ref[spot]], picked[spots_ref[spot + 1]]
                none = jnp.zeros_like(one)
                sources += [jnp.where(low16, one, none), jnp.where(low16, none, two)]
            each = lax.dot_general(
                jnp.concatenate(sources, axis=0),
                mats_ref[p],
                (((1,), (1,)), ((), ())),
                preferred_element_type=jnp.float32,
            )
            halves = [
                scale_ref[0, 2 * p + q] * each[2 * q * bands : (2 * q + 1) * bands]
                + scale_ref[1, 2 * p + q] * each[(2 * q + 1) * bands : (2 * q + 2) * bands]
                for q in range(2)
            ]
            both = jnp.where(low, halves[0], halves[1])
            mixed_ref[part, :, lanes] = (picked[p].astype(jnp.float32) + both).astype(jnp.bfloat16)

        tiles(part, at, one)

    for part in range(parts):
        over(part, gather)


def forward_kernel(starts_ref, keys_ref, weight_ref, mixed_ref, pert_ref, vert_ref, field_ref, obs_ref):
    levels, ncols = pert_ref.shape
    members = lax.axis_size("mem")
    wide, chunks, group = grouping(levels, ncols)
    rows = chunks * group
    scale_inv = 1.0 / math.sqrt(members)
    for c in range(chunks):
        part = slice(c * wide, (c + 1) * wide)
        mixed = mixed_ref[:, part]
        localized = mixed.astype(jnp.float32) + jnp.dot(
            vert_ref[...], mixed, preferred_element_type=jnp.float32
        )
        field = (pert_ref[:, part].astype(jnp.float32) * localized * scale_inv).astype(jnp.bfloat16)
        for g in range(levels // group):
            field_ref[g, c * group : (c + 1) * group, :] = field[g * group : (g + 1) * group, :]

    obs_ref[...] = jnp.zeros_like(obs_ref)
    nobs = weight_ref.shape[1]
    ncol = lax.axis_size("col")
    mine = lax.axis_index("col")

    def gathered(g, trip):
        runs = runs_of(starts_ref, g, mine, ncol)
        spans, rights, hots, rows_of = [], [], [], []
        for run in runs:
            which = run[0]
            span, valid = window_of(run, trip, nobs)
            width = width_of(which)
            lane = keys_ref[2 * which + 1 : 2 * which + 2, span]
            hots.append(one_hot(lane, row_numbers(wide, width), jnp.ones((1, width), jnp.bfloat16)))
            rows_of.append(jnp.where(valid, keys_ref[2 * which : 2 * which + 1, span], -1.0))
            weight = weight_ref[:, span]
            rights.append(1.0 - weight if which else weight)
            spans.append(span)
        hot = jnp.concatenate(hots, axis=1)
        lines = jnp.dot(field_ref[g], hot, preferred_element_type=jnp.float32).astype(jnp.bfloat16)
        at = 0
        for span, right, row in zip(spans, rights, rows_of):
            width = row.shape[1]
            kept = one_hot(row, row_numbers(rows, width), lines[:, at : at + width])
            found = kept[:SUBLANES]
            for r in range(SUBLANES, rows, SUBLANES):
                found = found + kept[r : r + SUBLANES]
            obs_ref[:, span] += right * jnp.sum(found.astype(jnp.float32), axis=0, keepdims=True)
            at += width

    for g in range(levels // group):
        gathered(g, 0)

    def collect(g, carry):
        def step(trip, carry):
            gathered(g, trip)
            return carry

        return lax.fori_loop(1, trips_of(runs_of(starts_ref, g, mine, ncol)), step, carry)

    lax.fori_loop(0, levels // group, collect, 0)


def finish_kernel(*refs, seen, group, wide):
    precision_ref, err_ref, guide_ref, image_ref, norm_ref = refs[:5]
    refs = refs[5:]
    seen_refs, refs = refs[:seen], refs[seen:]
    state_ref, field_ref = refs[-2:]
    refs = refs[:-2]
    steps = len(refs) // 4 + 1
    alphas, betas, rest = refs[: steps - 1], refs[steps - 1 : 2 * steps - 2], refs[2 * steps - 2 :]
    resids, fields = rest[:steps], rest[steps:]
    before = (guide_ref[...], image_ref[...], norm_ref[:, :1])
    alpha, beta, _, _, _ = advance(seen_refs, precision_ref[...], err_ref[...], before)
    alphas = [a[:, :1] for a in alphas] + [alpha]
    betas = [b[:, :1] for b in betas] + [beta]
    mix, shares = [], []
    for a, b in zip(alphas, betas):
        mix = [b * m for m in mix] + [jnp.ones_like(a)]
        shares = [s + a * m for s, m in zip(shares + [jnp.zeros_like(a)], mix)]
    state = shares[0] * resids[0][...]
    for share, resid in zip(shares[1:], resids[1:]):
        state = state + share * resid[...]
    state_ref[...] = state.astype(jnp.bfloat16)
    groups, rows, _ = fields[0].shape
    core = lax.axis_index("mem") % 2
    for g in range(groups):
        total = shares[0] * fields[0][g].astype(jnp.float32)
        for share, field in zip(shares[1:], fields[1:]):
            total = total + share * field[g].astype(jnp.float32)
        total = total.astype(jnp.bfloat16)
        for c in range(rows // group):
            part = slice(c * wide, (c + 1) * wide)
            if len(field_ref.shape) == 2:
                field_ref[g * group : (g + 1) * group, part] = total[c * group : (c + 1) * group, :]
            else:
                size = field_ref.shape[2]
                for s in range(group // size):
                    number = g * (group // size) + s
                    field_ref[(number % 2) ^ core, number // 2, :, part] = total[
                        c * group + s * size : c * group + (s + 1) * size, :
                    ]


def local_call(kernel, outs, args, name, scratch=(), scalars=1, remote=0):
    spaces = [pltpu.SMEM] * scalars + [pltpu.HBM] * remote + [pltpu.VMEM] * (len(args) - scalars - remote)
    kept = [
        a if space is pltpu.SMEM else pltpu.with_memory_space_constraint(a, space)
        for a, space in zip(args, spaces)
    ]
    return pl.pallas_call(
        kernel,
        out_shape=tuple(pltpu.VMEM(o.shape, o.dtype) for o in outs),
        in_specs=[pl.BlockSpec(memory_space=space) for space in spaces],
        out_specs=(pl.BlockSpec(memory_space=pltpu.VMEM),) * len(outs),
        scratch_shapes=list(scratch),
        compiler_params=pltpu.CompilerParams(vmem_limit_bytes=VMEM_BYTES),
        name=name,
    )(*kept)


def swap(x, axis, offset):
    n = lax.axis_size(axis)
    return lax.ppermute(x, axis, [(i, i ^ offset) for i in range(n)])


def total_over(x, axis, offsets):
    return sum([swap(x, axis, k).astype(jnp.float32) for k in offsets], x.astype(jnp.float32))


def shares_everywhere(x):
    shape = x.shape
    x = x.reshape(-1, LANES)
    x = total_over(x, "mem", (1,)).astype(jnp.bfloat16)
    x = total_over(x, "mem", range(2, lax.axis_size("mem"), 2)).astype(jnp.bfloat16)
    return [y.reshape(shape) for y in [x] + [swap(x, "col", k) for k in range(1, lax.axis_size("col"))]]


def scatter_members(field):
    if field.ndim == 2:
        nmem = lax.axis_size("mem")
        field = field.reshape(nmem, field.shape[0] // nmem, field.shape[1])
        pieces = lax.all_to_all(field, "mem", 0, 0, tiled=True)
        return jnp.sum(pieces.astype(jnp.float32), axis=0)
    mine = (field[0].astype(jnp.float32) + swap(field[1], "mem", 1).astype(jnp.float32)).astype(jnp.bfloat16)
    chips = mine.shape[0]
    chip = lax.axis_index("mem") // 2
    total = lax.dynamic_index_in_dim(mine, chip, 0, keepdims=False).astype(jnp.float32)
    for k in range(1, chips):
        piece = lax.dynamic_index_in_dim(mine, chip ^ k, 0, keepdims=False)
        total = total + swap(piece, "mem", 2 * k).astype(jnp.float32)
    return total


def per_device(
    perturbations,
    vertical,
    blocks,
    block_scale,
    block_cols,
    obs_level,
    obs_nodes,
    obs_weight,
    obs_value,
    obs_precision,
):
    local_members, levels, ncols = perturbations.shape
    assert local_members == 1
    nblocks, width, depth = blocks.shape
    assert 2 * width == LANES and depth == LANES
    ncol = lax.axis_size("col")
    nmem = lax.axis_size("mem")
    bands = levels // ncol
    pairs = nblocks // 2
    nodes = nblocks * width
    nobs = obs_level.shape[0]
    pert = perturbations[0]
    wide, chunks, group = grouping(levels, ncols)
    rows = chunks * group
    slices = levels // nmem

    level, node, other = obs_level, obs_nodes[:, 0], obs_nodes[:, 1]
    kind = ((level // group) * ncol + node // ncols) * ncol + other // ncols
    bounds = jnp.arange(levels // group * ncol * ncol + 1, dtype=jnp.int32)
    starts = jnp.sum((kind[None, :] < bounds[:, None]).astype(jnp.int32), axis=1)
    order = (kind * group + level % group) * ncols + node % ncols
    order, other, weight, value, precision = lax.sort(
        (order, other % ncols, obs_weight, obs_value, obs_precision), num_keys=1, is_stable=False
    )
    level = (order // ncols) % group
    keys = []
    for local in (order % ncols, other):
        keys += [(local // wide) * group + level, local % wide]
    keys = jnp.stack(keys).astype(jnp.float32)
    weight, value, precision = (a.reshape(1, nobs) for a in (weight, value, precision))

    tiles = min(TILES, ncols // LANES)
    mats = blocks.reshape(pairs, LANES, depth)
    which = jnp.arange(block_cols.shape[1], dtype=jnp.int32)[None, :]
    spots = (((block_cols & 1) ^ which) * pairs + (block_cols >> 1)).reshape(-1)

    vector = jax.ShapeDtypeStruct((1, nobs), jnp.float32)
    number = jax.ShapeDtypeStruct((1, LANES), jnp.float32)
    moved_shape = jax.ShapeDtypeStruct((ncol, bands, ncols), jnp.bfloat16)

    def adjoint(errors, seen, before):
        count = len(seen)
        outs = (moved_shape, vector) + ((number, number, vector, vector, number) if count else ())
        extra = (list(before) if before is not None else []) + list(seen)
        return local_call(
            functools.partial(adjoint_kernel, seen=count, first=before is None),
            outs,
            [starts, pert, vertical, keys, weight, precision, errors, *extra],
            "adjoint",
            [
                pltpu.VMEM((levels, ncols), jnp.float32),
                pltpu.VMEM((levels, ncols), jnp.bfloat16),
                pltpu.VMEM((levels, levels), jnp.bfloat16),
                pltpu.SemaphoreType.DMA((2,)),
            ],
            remote=2,
        )

    def middle(moved):
        vmem = pl.BlockSpec(memory_space=pltpu.VMEM)
        smem = pl.BlockSpec(memory_space=pltpu.SMEM)
        return pl.pallas_call(
            horizontal_kernel,
            out_shape=(
                pltpu.VMEM((bands, nodes), jnp.float32),
                pltpu.VMEM(moved_shape.shape, moved_shape.dtype),
            ),
            in_specs=[smem, smem, vmem, vmem],
            out_specs=(vmem, vmem),
            scratch_shapes=[
                pltpu.VMEM((2, 2 * tiles, bands, LANES), jnp.float32),
                pltpu.VMEM((2 * pairs, bands, LANES), jnp.float32),
                pltpu.VMEM((2 * pairs, bands, LANES), jnp.float32),
                pltpu.VMEM((2 * pairs, bands, LANES), jnp.bfloat16),
            ],
            compiler_params=pltpu.CompilerParams(vmem_limit_bytes=VMEM_BYTES),
            name="horizontal",
        )(
            spots,
            block_scale.T,
            pltpu.with_memory_space_constraint(moved, pltpu.VMEM),
            pltpu.with_memory_space_constraint(mats, pltpu.VMEM),
        )

    def forward(columns):
        field = jax.ShapeDtypeStruct((levels // group, rows, wide), jnp.bfloat16)
        return local_call(
            forward_kernel, (field, vector), [starts, keys, weight, columns, pert, vertical], "forward"
        )

    errors, seen, before = value, (), None
    alphas, betas, fields, resids = [], [], [], []
    for step in range(ITERS):
        if step == 0:
            sent, errors = adjoint(errors, seen, None)
        else:
            sent, errors, alpha, beta, *before = adjoint(errors, seen, before)
            alphas.append(alpha)
            betas.append(beta)
        moved = lax.all_to_all(sent, "col", 0, 0, tiled=True)
        resid, mixed = middle(moved)
        columns = lax.all_to_all(mixed, "col", 0, 0, tiled=True).reshape(levels, ncols)
        field, partial = forward(columns)
        seen = shares_everywhere(partial)
        resids.append(resid)
        fields.append(field)

    split = slices % 16 == 0 and group % slices == 0
    field_shape = (2, nmem // 2, slices, ncols) if split else (levels, ncols)
    args = [precision, errors, *before, *seen, *alphas, *betas, *resids, *fields]
    state, total = local_call(
        functools.partial(finish_kernel, seen=len(seen), group=group, wide=wide),
        (
            jax.ShapeDtypeStruct((bands, nodes), jnp.bfloat16),
            jax.ShapeDtypeStruct(field_shape, jnp.bfloat16),
        ),
        args,
        "finish",
        scalars=0,
    )
    return (state[None], scatter_members(total))


def solution(mesh):
    in_specs = (P("mem", None, "col"), P(), P(), P(), P(), P(), P(), P(), P(), P())
    out_specs = (P("mem", "col", None), P("mem", "col"))
    return jax.shard_map(
        per_device, mesh=mesh, in_specs=in_specs, out_specs=out_specs, check_vma=False
    )
```

```python
import functools
import math

import jax
import jax.numpy as jnp
from jax import lax
from jax.experimental import pallas as pl
from jax.experimental.pallas import tpu as pltpu
from jax.sharding import PartitionSpec as P

ITERS = 2
LANES = 128
SUBLANES = 16
WIDE = 256
ROWS = 256
FIRST = 768
SECOND = 384
TILES = 16
VMEM_BYTES = 24 << 20


def grouping(levels, ncols):
    wide = min(WIDE, ncols)
    chunks = ncols // wide
    group = max(8, min(levels, ROWS // chunks))
    return wide, chunks, group


def one_hot(keys, numbers, values):
    key = jnp.broadcast_to(keys.astype(jnp.bfloat16), numbers.shape)
    val = jnp.broadcast_to(values, numbers.shape)
    return jnp.where(numbers == key, val, jnp.zeros_like(val))


def row_numbers(rows, n):
    return lax.broadcasted_iota(jnp.int32, (rows, n), 0).astype(jnp.float32).astype(jnp.bfloat16)


def runs_of(starts_ref, g, mine, ncol):
    runs = [(0, starts_ref[(g * ncol + mine) * ncol], starts_ref[(g * ncol + mine + 1) * ncol])]
    for other in range(ncol):
        at = (g * ncol + other) * ncol + mine
        runs.append((1, starts_ref[at], starts_ref[at + 1]))
    return runs


def width_of(which):
    return SECOND if which else FIRST


def trips_of(runs):
    trips = jnp.int32(0)
    for which, low, end in runs:
        need = (end - (low // LANES) * LANES + width_of(which) - 1) // width_of(which)
        trips = jnp.maximum(trips, jnp.where(end > low, need, 0))
    return trips


def window_of(run, trip, nobs):
    which, low, end = run
    width = width_of(which)
    first = (low // LANES) * LANES + trip * width
    base = pl.multiple_of(jnp.minimum(first, nobs - width), LANES)
    place = base + lax.broadcasted_iota(jnp.int32, (1, width), 1)
    valid = (place >= jnp.maximum(low, first)) & (place < jnp.minimum(end, first + width))
    return pl.ds(base, width), valid


def total_of(x):
    return jnp.sum(x, axis=1, keepdims=True)


def advance(seen_refs, precision, errors, previous):
    seen = seen_refs[0][...].astype(jnp.float32)
    for ref in seen_refs[1:]:
        seen = seen + ref[...].astype(jnp.float32)
    norm = total_of(errors * seen)
    if previous is None:
        beta = jnp.zeros_like(norm)
        guide, image = errors, seen
    else:
        beta = norm / previous[2]
        guide, image = errors + beta * previous[0], seen + beta * previous[1]
    along = total_of(guide * image) + total_of(precision * image * image)
    return norm / along, beta, guide, image, norm


def adjoint_kernel(*refs, seen, first):
    starts_ref, pert_hbm, vert_hbm, keys_ref, weight_ref, precision_ref, err_ref = refs[:7]
    pert_ref, vert_ref, sems = refs[-3:]
    refs = refs[7:-3]
    levels, ncols = pert_ref.shape
    copies = [
        pltpu.make_async_copy(pert_hbm, pert_ref, sems.at[0]),
        pltpu.make_async_copy(vert_hbm, vert_ref, sems.at[1]),
    ]
    for copy in copies:
        copy.start()
    members = lax.axis_size("mem")
    wide, chunks, group = grouping(levels, ncols)
    rows = chunks * group
    if seen:
        before, refs = (None, refs) if first else ([r[...] for r in refs[:3]], refs[3:])
        seen_refs, refs = refs[:seen], refs[seen:]
        out_ref, new_ref, alpha_ref, beta_ref, guide_ref, image_ref, norm_ref, field = refs
        if before is not None:
            before[2] = before[2][:, :1]
        errors, precision = err_ref[...], precision_ref[...]
        alpha, beta, guide, image, norm = advance(seen_refs, precision, errors, before)
        new_ref[...] = errors - alpha * (guide + precision * image)
        guide_ref[...] = guide
        image_ref[...] = image
        for ref, value in ((alpha_ref, alpha), (beta_ref, beta), (norm_ref, norm)):
            ref[...] = jnp.broadcast_to(value, ref.shape)
    else:
        out_ref, new_ref, field = refs
        new_ref[...] = precision_ref[...] * err_ref[...]
    bands = out_ref.shape[1]
    nobs = weight_ref.shape[1]
    ncol = lax.axis_size("col")
    mine = lax.axis_index("col")

    def product(g, trip):
        above, beside = [], []
        for run in runs_of(starts_ref, g, mine, ncol):
            which = run[0]
            span, valid = window_of(run, trip, nobs)
            weight = weight_ref[:, span]
            weight = 1.0 - weight if which else weight
            row = jnp.where(valid, keys_ref[2 * which : 2 * which + 1, span], -1.0)
            lane = keys_ref[2 * which + 1 : 2 * which + 2, span]
            width = width_of(which)
            above.append(one_hot(row, row_numbers(rows, width), (weight * new_ref[:, span]).astype(jnp.bfloat16)))
            beside.append(one_hot(lane, row_numbers(wide, width), jnp.ones((1, width), jnp.bfloat16)))
        return lax.dot_general(
            jnp.concatenate(above, axis=1),
            jnp.concatenate(beside, axis=1),
            (((1,), (1,)), ((), ())),
            preferred_element_type=jnp.float32,
        )

    for g in range(levels // group):
        result = product(g, 0)
        for c in range(chunks):
            field[g * group : (g + 1) * group, c * wide : (c + 1) * wide] = result[c * group : (c + 1) * group]

    def collect(g, carry):
        here = pl.ds(pl.multiple_of(g * group, group), group)

        def step(trip, carry):
            result = product(g, trip)
            for c in range(chunks):
                field[here, c * wide : (c + 1) * wide] += result[c * group : (c + 1) * group]
            return carry

        return lax.fori_loop(1, trips_of(runs_of(starts_ref, g, mine, ncol)), step, carry)

    lax.fori_loop(0, levels // group, collect, 0)
    for copy in copies:
        copy.wait()
    scale_inv = 1.0 / math.sqrt(members)
    for c in range(chunks):
        part = slice(c * wide, (c + 1) * wide)
        scaled = (pert_ref[:, part].astype(jnp.float32) * field[:, part] * scale_inv).astype(jnp.bfloat16)
        turned = scaled.astype(jnp.float32) + lax.dot_general(
            vert_ref[...], scaled, (((0,), (0,)), ((), ())), preferred_element_type=jnp.float32
        )
        for b in range(out_ref.shape[0]):
            out_ref[b, :, part] = turned[b * bands : (b + 1) * bands, :].astype(jnp.bfloat16)


def horizontal_kernel(
    spots_ref, scale_ref, moved_ref, mats_ref, resid_ref, mixed_ref, terms, first, second, picked
):
    parts, bands, ncols = moved_ref.shape
    pairs = mats_ref.shape[0]
    per_part = ncols // LANES
    group = terms.shape[1] // 2
    half = LANES // 2
    lane = lax.broadcasted_iota(jnp.int32, (bands, LANES), 1)
    low = lane < half
    low16 = lane.astype(jnp.float32).astype(jnp.bfloat16) < half
    sums = (first, second)

    for s in sums:
        s[...] = jnp.zeros_like(s)

    def tiles(part, at, body):
        for u in range(group):
            lanes = pl.ds(pl.multiple_of((at + u) * LANES, LANES), LANES)
            body(u, part * per_part + at + u, lanes)

    def over(part, function):
        if per_part == group:
            function(part, 0, 0)
        else:
            lax.fori_loop(0, per_part // group, lambda n, c: function(part, n * group, n % 2) or c, 0)

    def products(part, at, slot):
        def one(u, p, lanes):
            tile = moved_ref[part, :, lanes]
            none = jnp.zeros_like(tile)
            tall = jnp.concatenate([jnp.where(low16, tile, none), jnp.where(low16, none, tile)], axis=0)
            both = jnp.dot(tall, mats_ref[p], preferred_element_type=jnp.float32)
            for q in range(2):
                scale = jnp.where(low[:1], scale_ref[0, 2 * p + q], scale_ref[1, 2 * p + q])
                terms[slot, 2 * u + q] = both[q * bands : (q + 1) * bands] * scale

        tiles(part, at, one)

    def scatter(base, slot):
        for n in range(2 * group):
            term = terms[slot, n]
            for k in range(2):
                sums[k][spots_ref[2 * base + 2 * n + k]] += term

    steps = per_part // group
    for part in range(parts):
        if steps == 1:
            products(part, 0, part % 2)
            if part > 0:
                scatter(2 * (part - 1) * per_part, (part - 1) % 2)
            continue
        products(part, 0, 0)

        def step(n, carry):
            scatter(2 * (part * per_part + (n - 1) * group), (n - 1) % 2)
            products(part, n * group, n % 2)
            return carry

        lax.fori_loop(1, steps, step, 0)
        scatter(2 * (part * per_part + (steps - 1) * group), (steps - 1) % 2)
    if steps == 1:
        scatter(2 * (parts - 1) * per_part, (parts - 1) % 2)

    def join(part, at, slot):
        def one(u, p, lanes):
            here = jnp.where(low, first[p], second[p])
            there = jnp.where(low, first[pairs + p], second[pairs + p])
            resid = moved_ref[part, :, lanes].astype(jnp.float32) + here + pltpu.roll(there, half, 1)
            resid_ref[:, pl.ds(pl.multiple_of(p * LANES, LANES), LANES)] = resid
            picked[p] = resid.astype(jnp.bfloat16)
            picked[pairs + p] = pltpu.roll(resid, half, 1).astype(jnp.bfloat16)

        tiles(part, at, one)

    for part in range(parts):
        over(part, join)

    def gather(part, at, slot):
        base = 4 * (part * per_part + at)

        def one(u, p, lanes):
            sources = []
            for q in range(2):
                spot = base + 4 * u + 2 * q
                one, two = picked[spots_ref[spot]], picked[spots_ref[spot + 1]]
                none = jnp.zeros_like(one)
                sources += [jnp.where(low16, one, none), jnp.where(low16, none, two)]
            each = lax.dot_general(
                jnp.concatenate(sources, axis=0),
                mats_ref[p],
                (((1,), (1,)), ((), ())),
                preferred_element_type=jnp.float32,
            )
            halves = [
                scale_ref[0, 2 * p + q] * each[2 * q * bands : (2 * q + 1) * bands]
                + scale_ref[1, 2 * p + q] * each[(2 * q + 1) * bands : (2 * q + 2) * bands]
                for q in range(2)
            ]
            both = jnp.where(low, halves[0], halves[1])
            mixed_ref[part, :, lanes] = (picked[p].astype(jnp.float32) + both).astype(jnp.bfloat16)

        tiles(part, at, one)

    for part in range(parts):
        over(part, gather)


def forward_kernel(starts_ref, keys_ref, weight_ref, mixed_ref, pert_ref, vert_ref, field_ref, obs_ref):
    levels, ncols = pert_ref.shape
    members = lax.axis_size("mem")
    wide, chunks, group = grouping(levels, ncols)
    rows = chunks * group
    scale_inv = 1.0 / math.sqrt(members)
    for c in range(chunks):
        part = slice(c * wide, (c + 1) * wide)
        mixed = mixed_ref[:, part]
        localized = mixed.astype(jnp.float32) + jnp.dot(
            vert_ref[...], mixed, preferred_element_type=jnp.float32
        )
        field = (pert_ref[:, part].astype(jnp.float32) * localized * scale_inv).astype(jnp.bfloat16)
        for g in range(levels // group):
            field_ref[g, c * group : (c + 1) * group, :] = field[g * group : (g + 1) * group, :]

    obs_ref[...] = jnp.zeros_like(obs_ref)
    nobs = weight_ref.shape[1]
    ncol = lax.axis_size("col")
    mine = lax.axis_index("col")

    def gathered(g, trip):
        runs = runs_of(starts_ref, g, mine, ncol)
        spans, rights, hots, rows_of = [], [], [], []
        for run in runs:
            which = run[0]
            span, valid = window_of(run, trip, nobs)
            width = width_of(which)
            lane = keys_ref[2 * which + 1 : 2 * which + 2, span]
            hots.append(one_hot(lane, row_numbers(wide, width), jnp.ones((1, width), jnp.bfloat16)))
            rows_of.append(jnp.where(valid, keys_ref[2 * which : 2 * which + 1, span], -1.0))
            weight = weight_ref[:, span]
            rights.append(1.0 - weight if which else weight)
            spans.append(span)
        hot = jnp.concatenate(hots, axis=1)
        lines = jnp.dot(field_ref[g], hot, preferred_element_type=jnp.float32).astype(jnp.bfloat16)
        at = 0
        for span, right, row in zip(spans, rights, rows_of):
            width = row.shape[1]
            kept = one_hot(row, row_numbers(rows, width), lines[:, at : at + width])
            found = kept[:SUBLANES]
            for r in range(SUBLANES, rows, SUBLANES):
                found = found + kept[r : r + SUBLANES]
            obs_ref[:, span] += right * jnp.sum(found.astype(jnp.float32), axis=0, keepdims=True)
            at += width

    for g in range(levels // group):
        gathered(g, 0)

    def collect(g, carry):
        def step(trip, carry):
            gathered(g, trip)
            return carry

        return lax.fori_loop(1, trips_of(runs_of(starts_ref, g, mine, ncol)), step, carry)

    lax.fori_loop(0, levels // group, collect, 0)


def finish_kernel(*refs, seen, group, wide):
    precision_ref, err_ref, guide_ref, image_ref, norm_ref = refs[:5]
    refs = refs[5:]
    seen_refs, refs = refs[:seen], refs[seen:]
    state_ref, field_ref = refs[-2:]
    refs = refs[:-2]
    steps = len(refs) // 4 + 1
    alphas, betas, rest = refs[: steps - 1], refs[steps - 1 : 2 * steps - 2], refs[2 * steps - 2 :]
    resids, fields = rest[:steps], rest[steps:]
    before = (guide_ref[...], image_ref[...], norm_ref[:, :1])
    alpha, beta, _, _, _ = advance(seen_refs, precision_ref[...], err_ref[...], before)
    alphas = [a[:, :1] for a in alphas] + [alpha]
    betas = [b[:, :1] for b in betas] + [beta]
    mix, shares = [], []
    for a, b in zip(alphas, betas):
        mix = [b * m for m in mix] + [jnp.ones_like(a)]
        shares = [s + a * m for s, m in zip(shares + [jnp.zeros_like(a)], mix)]
    state = shares[0] * resids[0][...]
    for share, resid in zip(shares[1:], resids[1:]):
        state = state + share * resid[...]
    state_ref[...] = state.astype(jnp.bfloat16)
    groups, rows, _ = fields[0].shape
    core = lax.axis_index("mem") % 2
    for g in range(groups):
        total = shares[0] * fields[0][g].astype(jnp.float32)
        for share, field in zip(shares[1:], fields[1:]):
            total = total + share * field[g].astype(jnp.float32)
        total = total.astype(jnp.bfloat16)
        for c in range(rows // group):
            part = slice(c * wide, (c + 1) * wide)
            if len(field_ref.shape) == 2:
                field_ref[g * group : (g + 1) * group, part] = total[c * group : (c + 1) * group, :]
            else:
                size = field_ref.shape[2]
                for s in range(group // size):
                    number = g * (group // size) + s
                    field_ref[(number % 2) ^ core, number // 2, :, part] = total[
                        c * group + s * size : c * group + (s + 1) * size, :
                    ]


def local_call(kernel, outs, args, name, scratch=(), scalars=1, remote=0):
    spaces = [pltpu.SMEM] * scalars + [pltpu.HBM] * remote + [pltpu.VMEM] * (len(args) - scalars - remote)
    kept = [
        a if space is pltpu.SMEM else pltpu.with_memory_space_constraint(a, space)
        for a, space in zip(args, spaces)
    ]
    return pl.pallas_call(
        kernel,
        out_shape=tuple(pltpu.VMEM(o.shape, o.dtype) for o in outs),
        in_specs=[pl.BlockSpec(memory_space=space) for space in spaces],
        out_specs=(pl.BlockSpec(memory_space=pltpu.VMEM),) * len(outs),
        scratch_shapes=list(scratch),
        compiler_params=pltpu.CompilerParams(vmem_limit_bytes=VMEM_BYTES),
        name=name,
    )(*kept)


def swap(x, axis, offset):
    n = lax.axis_size(axis)
    return lax.ppermute(x, axis, [(i, i ^ offset) for i in range(n)])


def total_over(x, axis, offsets):
    return sum([swap(x, axis, k).astype(jnp.float32) for k in offsets], x.astype(jnp.float32))


def shares_everywhere(x):
    shape = x.shape
    x = x.reshape(-1, LANES)
    x = total_over(x, "mem", (1,)).astype(jnp.bfloat16)
    x = total_over(x, "col", range(1, lax.axis_size("col"))).astype(jnp.bfloat16)
    ring = range(2, lax.axis_size("mem"), 2)
    return [y.reshape(shape) for y in [x] + [swap(x, "mem", k) for k in ring]]


def scatter_members(field):
    if field.ndim == 2:
        nmem = lax.axis_size("mem")
        field = field.reshape(nmem, field.shape[0] // nmem, field.shape[1])
        pieces = lax.all_to_all(field, "mem", 0, 0, tiled=True)
        return jnp.sum(pieces.astype(jnp.float32), axis=0)
    mine = (field[0].astype(jnp.float32) + swap(field[1], "mem", 1).astype(jnp.float32)).astype(jnp.bfloat16)
    chips = mine.shape[0]
    chip = lax.axis_index("mem") // 2
    total = lax.dynamic_index_in_dim(mine, chip, 0, keepdims=False).astype(jnp.float32)
    for k in range(1, chips):
        piece = lax.dynamic_index_in_dim(mine, chip ^ k, 0, keepdims=False)
        total = total + swap(piece, "mem", 2 * k).astype(jnp.float32)
    return total


def per_device(
    perturbations,
    vertical,
    blocks,
    block_scale,
    block_cols,
    obs_level,
    obs_nodes,
    obs_weight,
    obs_value,
    obs_precision,
):
    local_members, levels, ncols = perturbations.shape
    assert local_members == 1
    nblocks, width, depth = blocks.shape
    assert 2 * width == LANES and depth == LANES
    ncol = lax.axis_size("col")
    nmem = lax.axis_size("mem")
    bands = levels // ncol
    pairs = nblocks // 2
    nodes = nblocks * width
    nobs = obs_level.shape[0]
    pert = perturbations[0]
    wide, chunks, group = grouping(levels, ncols)
    rows = chunks * group
    slices = levels // nmem

    level, node, other = obs_level, obs_nodes[:, 0], obs_nodes[:, 1]
    kind = ((level // group) * ncol + node // ncols) * ncol + other // ncols
    bounds = jnp.arange(levels // group * ncol * ncol + 1, dtype=jnp.int32)
    starts = jnp.sum((kind[None, :] < bounds[:, None]).astype(jnp.int32), axis=1)
    order = (kind * group + level % group) * ncols + node % ncols
    order, other, weight, value, precision = lax.sort(
        (order, other % ncols, obs_weight, obs_value, obs_precision), num_keys=1, is_stable=False
    )
    level = (order // ncols) % group
    keys = []
    for local in (order % ncols, other):
        keys += [(local // wide) * group + level, local % wide]
    keys = jnp.stack(keys).astype(jnp.float32)
    weight, value, precision = (a.reshape(1, nobs) for a in (weight, value, precision))

    tiles = min(TILES, ncols // LANES)
    mats = blocks.reshape(pairs, LANES, depth)
    which = jnp.arange(block_cols.shape[1], dtype=jnp.int32)[None, :]
    spots = (((block_cols & 1) ^ which) * pairs + (block_cols >> 1)).reshape(-1)

    vector = jax.ShapeDtypeStruct((1, nobs), jnp.float32)
    number = jax.ShapeDtypeStruct((1, LANES), jnp.float32)
    moved_shape = jax.ShapeDtypeStruct((ncol, bands, ncols), jnp.bfloat16)

    def adjoint(errors, seen, before):
        count = len(seen)
        outs = (moved_shape, vector) + ((number, number, vector, vector, number) if count else ())
        extra = (list(before) if before is not None else []) + list(seen)
        return local_call(
            functools.partial(adjoint_kernel, seen=count, first=before is None),
            outs,
            [starts, pert, vertical, keys, weight, precision, errors, *extra],
            "adjoint",
            [
                pltpu.VMEM((levels, ncols), jnp.float32),
                pltpu.VMEM((levels, ncols), jnp.bfloat16),
                pltpu.VMEM((levels, levels), jnp.bfloat16),
                pltpu.SemaphoreType.DMA((2,)),
            ],
            remote=2,
        )

    def middle(moved):
        vmem = pl.BlockSpec(memory_space=pltpu.VMEM)
        smem = pl.BlockSpec(memory_space=pltpu.SMEM)
        return pl.pallas_call(
            horizontal_kernel,
            out_shape=(
                pltpu.VMEM((bands, nodes), jnp.float32),
                pltpu.VMEM(moved_shape.shape, moved_shape.dtype),
            ),
            in_specs=[smem, smem, vmem, vmem],
            out_specs=(vmem, vmem),
            scratch_shapes=[
                pltpu.VMEM((2, 2 * tiles, bands, LANES), jnp.float32),
                pltpu.VMEM((2 * pairs, bands, LANES), jnp.float32),
                pltpu.VMEM((2 * pairs, bands, LANES), jnp.float32),
                pltpu.VMEM((2 * pairs, bands, LANES), jnp.bfloat16),
            ],
            compiler_params=pltpu.CompilerParams(vmem_limit_bytes=VMEM_BYTES),
            name="horizontal",
        )(
            spots,
            block_scale.T,
            pltpu.with_memory_space_constraint(moved, pltpu.VMEM),
            pltpu.with_memory_space_constraint(mats, pltpu.VMEM),
        )

    def forward(columns):
        field = jax.ShapeDtypeStruct((levels // group, rows, wide), jnp.bfloat16)
        return local_call(
            forward_kernel, (field, vector), [starts, keys, weight, columns, pert, vertical], "forward"
        )

    errors, seen, before = value, (), None
    alphas, betas, fields, resids = [], [], [], []
    for step in range(ITERS):
        if step == 0:
            sent, errors = adjoint(errors, seen, None)
        else:
            sent, errors, alpha, beta, *before = adjoint(errors, seen, before)
            alphas.append(alpha)
            betas.append(beta)
        moved = lax.all_to_all(sent, "col", 0, 0, tiled=True)
        resid, mixed = middle(moved)
        columns = lax.all_to_all(mixed, "col", 0, 0, tiled=True).reshape(levels, ncols)
        field, partial = forward(columns)
        seen = shares_everywhere(partial)
        resids.append(resid)
        fields.append(field)

    split = slices % 16 == 0 and group % slices == 0
    field_shape = (2, nmem // 2, slices, ncols) if split else (levels, ncols)
    args = [precision, errors, *before, *seen, *alphas, *betas, *resids, *fields]
    state, total = local_call(
        functools.partial(finish_kernel, seen=len(seen), group=group, wide=wide),
        (
            jax.ShapeDtypeStruct((bands, nodes), jnp.bfloat16),
            jax.ShapeDtypeStruct(field_shape, jnp.bfloat16),
        ),
        args,
        "finish",
        scalars=0,
    )
    return (state[None], scatter_members(total))


def solution(mesh):
    in_specs = (P("mem", None, "col"), P(), P(), P(), P(), P(), P(), P(), P(), P())
    out_specs = (P("mem", "col", None), P("mem", "col"))
    return jax.shard_map(
        per_device, mesh=mesh, in_specs=in_specs, out_specs=out_specs, check_vma=False
    )
```
